256 devices in a mesh: dp: 16 (over y, x), mem: 16 (over z, core).
Axes of the slice: x: 4, y: 4, z: 8, core: 2. Of those that a mesh axis runs over, the one named last changes fastest.
Arguments:
- grad_out: bfloat16 [2048, 4096], P('dp', 'mem'), may hold values from -16 to 16
- values: bfloat16 [4096, 4096], P('dp', 'mem'), may hold values from -0.0234375 to 0.0234375
- slot_rows: int32 [2048, 32], P('dp'), may hold values from 0 to 4095, all different within a row
- weights: float32 [2048, 32], P('dp'), may hold values from 0 to 1, as said below
- sub_picks: int32 [2, 2048, 32], P(None, 'dp'), may hold values from 0 to 1023
- queries: bfloat16 [2048, 1024], P('dp'), may hold values from -6 to 6
- sub_keys: bfloat16 [2, 1024, 512], replicated, may hold values from -0.25 to 0.25
- layer_input: bfloat16 [2048, 4096], P('dp', 'mem'), may hold values from -6 to 6
Outputs:
- value_grad: float32 [4096, 4096], P('dp', 'mem')
- key_grad: float32 [2, 1024, 512], P(None, 'dp')
- proj_grad: float32 [1024, 4096], P('dp', 'mem')
The draws below stay inside these ranges and needn't reach their ends.
Inputs may be any that keep to these rules, and one draw needn't show every extreme that they name: `slot_rows`: the 32 value rows of one token are distinct, and every value row is read by some token. Each token's 32 weights are positive and sum to one.
All inputs are finite; a program needn't handle non-finite values.
Results may differ from the reference program's by a relative error of at most 0.004.
Values may be sent and summed in bfloat16 or wider, within the bound.
No kernel may reach another device: no remote copies, remote signals or barrier semaphores. Data moves between devices by JAX's collectives and lax.ppermute only.
A program may use at most 64 MiB of HBM per device.

```python
import jax
import jax.numpy as jnp
from jax import lax

D = 4096
SUB = 1024
KDIM = 512
TOPK = 32
TOKENS = 2048
NVAL = 4096


def draw_weights(key, part):
    logits = jax.random.normal(key, (TOKENS, TOPK), jnp.float32) * 1.5
    raised = jnp.exp(logits)
    return raised / jnp.sum(raised, axis=1, keepdims=True)


def with_ends(values, rng, least, top_value):
    longest = values.shape.index(max(values.shape))
    spots = []
    for shift in (0, 1):
        where = [jax.random.randint(jax.random.fold_in(rng, axis), (), 0, length) for axis, length in enumerate(values.shape)]
        where[longest] = (where[longest] + shift) % values.shape[longest]
        spots.append(tuple(where))
    return values.at[spots[0]].set(least).at[spots[1]].set(top_value)


def block_levels(rng, dims, cuts, smallest, high):
    loudness = 1.0
    for axis_at, blocks in cuts:
        steps = jax.random.uniform(jax.random.fold_in(jax.random.fold_in(rng, 6), axis_at), (blocks,), jnp.float32, smallest / len(cuts), high / len(cuts))
        loudness = loudness * jnp.repeat(jnp.exp(steps), dims[axis_at] // blocks).reshape((-1,) + (1,) * (len(dims) - 1 - axis_at))
    return loudness


def picks_of(own_key, rows, amount, top, lift):
    ranking = jax.random.permutation(jax.random.fold_in(own_key, 1), amount)
    boost = ranking
    for power in range(3):
        boost = boost * boost // amount
    boost = boost * lift // amount
    chance = jax.random.randint(jax.random.fold_in(own_key, 2), (rows, amount), 0, 4096) + boost
    sure = jax.random.permutation(jax.random.fold_in(own_key, 3), rows)[jnp.arange(amount) % rows]
    chance = jnp.where(jnp.arange(rows)[:, None] == sure[None, :], 1 << 14, chance)
    score = chance * amount + jnp.arange(amount)
    return lax.top_k(score.astype(jnp.int32), top)[1].astype(jnp.int32)


def noise(rng, shape, width, limit, pieces=(), held_as=jnp.bfloat16):
    factor_of = block_levels(rng, shape, pieces, -0.22, 0.18) if pieces else 1.0
    array = jax.random.normal(rng, shape, jnp.float32) * width * factor_of
    return jnp.minimum(jnp.maximum(array, -limit), limit).astype(held_as)


def setup_inputs(seed: int = 0) -> dict:
    key_list = jax.random.split(jax.random.key(seed), 9)
    grad_out = noise(key_list[0], (TOKENS, D), 4.0, 16.0, ((0, 16), (1, 16)))
    values = noise(key_list[1], (NVAL, D), (16 * D) ** -0.5, 0.0234375, ((0, 16), (1, 16)))
    slot_rows = picks_of(key_list[2], TOKENS, NVAL, TOPK, 128)
    weights = draw_weights(jax.random.fold_in(key_list[8], 71), 0)
    sub_picks = with_ends(jax.random.randint(key_list[4], (2, TOKENS, TOPK), 0, SUB), jax.random.fold_in(key_list[4], 1), 0, SUB - 1).astype(jnp.int32)
    queries = noise(key_list[5], (TOKENS, 2 * KDIM), 1.0, 6.0, ((0, 16),))
    sub_keys = noise(key_list[6], (2, SUB, KDIM), KDIM ** -0.5, 0.25)
    layer_input = noise(key_list[7], (TOKENS, D), 1.0, 6.0, ((0, 16), (1, 16)))
    return {"grad_out": grad_out, "values": values, "slot_rows": slot_rows, "weights": weights, "sub_picks": sub_picks, "queries": queries, "sub_keys": sub_keys, "layer_input": layer_input}


def reference(grad_out, values, slot_rows, weights, sub_picks, queries, sub_keys, layer_input):
    vweights = weights.astype(jnp.bfloat16).astype(jnp.float32)
    grad_wide = grad_out.astype(jnp.float32)

    def add_slot(slot_index, running):
        value_grad, slot_grad = running
        slot_at = jnp.asarray(slot_index).astype(jnp.int32)
        rows_now = lax.dynamic_slice_in_dim(slot_rows, slot_at, 1, 1)[:, 0]
        weight_now = lax.dynamic_slice_in_dim(vweights, slot_at, 1, 1)
        value_grad = value_grad.at[rows_now].add(weight_now * grad_wide)
        fetched = jnp.take(values, rows_now, axis=0).astype(jnp.float32)
        inner_sums = jnp.sum(fetched * grad_wide, axis=1, keepdims=True)
        slot_grad = lax.dynamic_update_slice_in_dim(slot_grad, inner_sums, slot_at, 1)
        return value_grad, slot_grad

    start_values = jnp.zeros((NVAL, D), jnp.float32)
    start_slots = jnp.zeros((TOKENS, TOPK), jnp.float32)
    value_grad, slot_grad = lax.fori_loop(0, TOPK, add_slot, (start_values, start_slots))
    centered = slot_grad - jnp.sum(weights * slot_grad, axis=1, keepdims=True)
    score_grad = weights * centered
    token_ids = jnp.arange(TOKENS, dtype=jnp.int32)[:, None]
    halves = []
    for half_index in range(2):
        summed = jnp.zeros((TOKENS, SUB), jnp.float32).at[token_ids, sub_picks[half_index]].add(score_grad)
        halves.append(summed.astype(jnp.bfloat16))
    key_parts = []
    query_parts = []
    for half_index in range(2):
        query_half = queries[:, half_index * KDIM:(half_index + 1) * KDIM]
        key_parts.append(jnp.dot(halves[half_index].T, query_half, preferred_element_type=jnp.float32))
        query_parts.append(jnp.dot(halves[half_index], sub_keys[half_index], preferred_element_type=jnp.float32))
    key_grad = jnp.stack(key_parts, axis=0)
    dquery = jnp.concatenate(query_parts, axis=1).astype(jnp.bfloat16)
    proj_grad = jnp.dot(dquery.T, layer_input, preferred_element_type=jnp.float32)
    return value_grad, key_grad, proj_grad
```

```python
import jax
import jax.numpy as jnp
from jax import lax
from jax.experimental import pallas as pl
from jax.experimental.pallas import tpu as pltpu
from jax.sharding import PartitionSpec as P


f32 = jnp.float32
bf16 = jnp.bfloat16
VM = pl.BlockSpec(memory_space=pltpu.VMEM)


def run(kernel, outs, args, scratch=(), flops=0, data=0):
    return pl.pallas_call(
        kernel,
        out_shape=outs,
        in_specs=[VM] * len(args),
        out_specs=jax.tree.map(lambda _: VM, outs),
        scratch_shapes=list(scratch),
        cost_estimate=pl.CostEstimate(flops=flops, bytes_accessed=data, transcendentals=0),
    )(*args)


def shape(dims, dtype):
    return jax.ShapeDtypeStruct(dims, dtype)


def pack_kernel(grad_ref, rows_ref, weights_ref, out_ref):
    ids = rows_ref[...]
    power = ids >> 7
    scale = (1 << (power & 15)).astype(f32) * jnp.where(power >= 16, 65536.0, 1.0)
    codes = ((ids & 127) + 128).astype(f32) * scale
    both = jnp.concatenate([codes.T, weights_ref[...].T], axis=1).astype(bf16)
    grads = grad_ref[...]
    tokens = grads.shape[0]
    for at in range(out_ref.shape[0]):
        out_ref[at, :tokens, :] = grads
        out_ref[at, tokens:, :] = both


def local_rows(codes):
    owner = lax.axis_index("dp")
    scale = jnp.float32(1.0)
    for bit in range(4):
        scale = scale * jnp.where((owner >> bit) & 1 == 1, 0.25 ** (2**bit), 1.0)
    moved = codes.astype(f32) * scale
    row = jnp.where(moved < 256.0, moved - 128.0, moved * 0.5)
    return jnp.where((moved >= 128.0) & (moved < 512.0), row, -1.0)


def slot_kernel(recv_ref, values_ref, out_ref):
    sources, slots, tokens = out_ref.shape
    val_rows = values_ref.shape[0]

    def one(at, carry):
        grads = recv_ref[at, :tokens, :]
        scores = lax.dot_general(
            values_ref[...], grads, (((1,), (1,)), ((), ())), preferred_element_type=f32
        )
        row = local_rows(recv_ref[at, tokens:, :tokens]).astype(jnp.int32)
        high = row >> 3
        low = row & 7
        for part in range(slots // 8):
            mine = slice(part * 8, part * 8 + 8)
            low_now, high_now = low[mine], high[mine]
            acc = jnp.zeros((8, tokens), f32)
            for tile in range(val_rows // 8):
                got = jnp.take_along_axis(scores[tile * 8 : tile * 8 + 8], low_now, axis=0)
                acc = jnp.where(high_now == tile, got, acc)
            out_ref[at, mine, :] = acc
        return carry

    lax.fori_loop(0, sources, one, 0)


def value_kernel(recv_ref, out_ref, rows_ref, wide_ref, bag_ref, grads_ref):
    sources = recv_ref.shape[0]
    val_rows = out_ref.shape[0]
    tokens = bag_ref.shape[1] // sources
    slots = recv_ref.shape[1] - tokens
    iota = lax.broadcasted_iota(jnp.int32, (val_rows, tokens), 0).astype(f32)

    def one(at, carry):
        span = pl.ds(pl.multiple_of(at * tokens, tokens), tokens)
        rows_ref[...] = local_rows(recv_ref[at, tokens:, :tokens])
        wide_ref[...] = recv_ref[at, tokens:, tokens:].astype(f32)
        grads_ref[span, :] = recv_ref[at, :tokens, :]
        for block in range(val_rows // 128):
            acc = jnp.zeros((128, tokens), f32)
            ids = iota[block * 128 : block * 128 + 128]
            for slot in range(slots):
                hit = ids == rows_ref[slot : slot + 1, :]
                acc = jnp.where(hit, wide_ref[slot : slot + 1, :], acc)
            bag_ref[block * 128 : block * 128 + 128, span] = acc.astype(bf16)
        return carry

    lax.fori_loop(0, sources, one, 0)
    out_ref[...] = jnp.dot(bag_ref[...], grads_ref[...], preferred_element_type=f32)


def part_kernel(
    slot_ref, weights_ref, picks_ref, queries_ref, keys_ref, layer_ref, out_ref, score_ref, sub_ref
):
    slots, tokens = slot_ref.shape
    halves, subs, width = keys_ref.shape
    quarter = lax.axis_index("mem") & 3
    weights = weights_ref[...]
    slot_grad = slot_ref[...]
    centered = slot_grad - jnp.sum(weights * slot_grad, axis=0, keepdims=True)
    score_ref[...] = weights * centered
    block = 64
    iota = lax.broadcasted_iota(jnp.int32, (block, tokens), 0)
    for half in range(halves):

        def one(at, carry, half=half):
            start = pl.multiple_of(at * block, block)
            ids = iota + start
            acc = jnp.zeros((block, tokens), f32)
            for slot in range(slots):
                hit = ids == picks_ref[half, slot : slot + 1, :]
                acc = acc + jnp.where(hit, score_ref[slot : slot + 1, :], 0.0)
            sub_ref[half, pl.ds(start, block), :] = acc.astype(bf16)
            return carry

        lax.fori_loop(0, subs // block, one, 0)
    dests = out_ref.shape[0]
    own = subs // dests
    layer = layer_ref[...]
    for half in range(halves):
        dquery = lax.dot_general(
            sub_ref[half], keys_ref[half], (((0,), (0,)), ((), ())), preferred_element_type=f32
        ).astype(bf16)
        proj = lax.dot_general(
            dquery, layer, (((0,), (0,)), ((), ())), preferred_element_type=f32
        ).astype(bf16)
        per = width // own
        for at in range(per):
            out_ref[half * per + at, :own, :] = proj[at * own : at * own + own]
    cut = queries_ref.shape[1] // 4
    mine = queries_ref[:, pl.ds(pl.multiple_of(quarter * cut, cut), cut)]
    key = jnp.dot(sub_ref[quarter >> 1], mine, preferred_element_type=f32).astype(bf16)
    for at in range(dests):
        out_ref[at, own:, :] = key[at * own : at * own + own]


def sum_kernel(parts_ref, proj_ref, key_ref):
    own = proj_ref.shape[0]
    total = parts_ref[0].astype(f32)
    for at in range(1, parts_ref.shape[0]):
        total = total + parts_ref[at].astype(f32)
    proj_ref[...] = total[:own]
    key_ref[...] = total[own:]


def join_kernel(own_ref, one_ref, two_ref, three_ref, out_ref):
    quarter = lax.axis_index("mem") & 3
    cut = own_ref.shape[1]
    for at, ref in enumerate((own_ref, one_ref, two_ref, three_ref)):
        there = quarter ^ at
        out_ref[there >> 1, :, pl.ds(pl.multiple_of((there & 1) * cut, cut), cut)] = ref[...]


def swap(x, mask, count):
    return lax.ppermute(x, "mem", [(at, at ^ mask) for at in range(count)])


def body(grad_out, values, slot_rows, weights, sub_picks, queries, sub_keys, layer_input):
    groups = lax.axis_size("dp")
    mem_count = lax.axis_size("mem")
    tokens, width = grad_out.shape
    slots = slot_rows.shape[1]
    val_rows = values.shape[0]
    halves, subs, key_width = sub_keys.shape
    weights_t = weights.T
    picks_t = jnp.swapaxes(sub_picks, 1, 2)

    sent = run(
        pack_kernel, shape((groups, tokens + slots, width), bf16), (grad_out, slot_rows, weights)
    )
    recv = lax.all_to_all(sent, "dp", 0, 0, tiled=True)
    slot_parts = run(slot_kernel, shape((groups, slots, tokens), f32), (recv, values))
    slot_parts = lax.all_to_all(slot_parts, "dp", 0, 0, tiled=True)
    slot_grad = jnp.sum(slot_parts, axis=0)

    value_grad = run(
        value_kernel,
        shape((val_rows, width), f32),
        (recv,),
        scratch=(
            pltpu.VMEM((slots, tokens), f32),
            pltpu.VMEM((slots, tokens), f32),
            pltpu.VMEM((val_rows, groups * tokens), bf16),
            pltpu.VMEM((groups * tokens, width), bf16),
        ),
        flops=4 * 10**9,
        data=2**21,
    )
    for step in (1, 4):
        one = swap(slot_grad, step, mem_count)
        two = swap(slot_grad, 2 * step, mem_count)
        three = swap(slot_grad, 3 * step, mem_count)
        slot_grad = (slot_grad + one) + (two + three)

    own = subs // groups
    parts = run(
        part_kernel,
        shape((groups, 2 * own, width), bf16),
        (slot_grad, weights_t, picks_t, queries, sub_keys, layer_input),
        scratch=(pltpu.VMEM((slots, tokens), f32), pltpu.VMEM((halves, subs, tokens), bf16)),
    )
    parts = lax.all_to_all(parts, "dp", 0, 0, tiled=True)
    proj_grad, key = run(sum_kernel, (shape((own, width), f32), shape((own, width), f32)), (parts,))
    others = [swap(key, mask, mem_count) for mask in (1, 2, 3)]
    key_grad = run(join_kernel, shape((halves, own, key_width), f32), (key, *others))
    return (value_grad, key_grad, proj_grad)


def solution(mesh):
    return jax.shard_map(
        body,
        mesh=mesh,
        in_specs=(
            P("dp", "mem"),
            P("dp", "mem"),
            P("dp", None),
            P("dp", None),
            P(None, "dp", None),
            P("dp", None),
            P(),
            P("dp", "mem"),
        ),
        out_specs=(P("dp", "mem"), P(None, "dp", None), P("dp", "mem")),
        check_vma=False,
    )
```

```python
import functools

import jax
import jax.numpy as jnp
from jax import lax
from jax.experimental import pallas as pl
from jax.experimental.pallas import tpu as pltpu
from jax.sharding import PartitionSpec as P


f32 = jnp.float32
bf16 = jnp.bfloat16
VM = pl.BlockSpec(memory_space=pltpu.VMEM)
ANY = pl.BlockSpec(memory_space=pl.ANY)


def run(kernel, outs, args, scratch=(), flops=0, data=0, far=()):
    return pl.pallas_call(
        kernel,
        out_shape=outs,
        in_specs=[ANY if at in far else VM for at in range(len(args))],
        out_specs=jax.tree.map(lambda _: VM, outs),
        scratch_shapes=list(scratch),
        cost_estimate=pl.CostEstimate(flops=flops, bytes_accessed=data, transcendentals=0),
        compiler_params=pltpu.CompilerParams(vmem_limit_bytes=16 * 2**20),
    )(*args)


def shape(dims, dtype):
    return jax.ShapeDtypeStruct(dims, dtype)


def pack_kernel(grad_ref, rows_ref, weights_ref, out_ref):
    ids = rows_ref[...]
    power = ids >> 7
    scale = (1 << (power & 15)).astype(f32) * jnp.where(power >= 16, 65536.0, 1.0)
    codes = ((ids & 127) + 128).astype(f32) * scale
    both = jnp.concatenate([codes, weights_ref[...]], axis=1).astype(bf16)
    grads = grad_ref[...]
    tokens = grads.shape[0]
    for at in range(out_ref.shape[0]):
        out_ref[at, :tokens, :] = grads
        out_ref[at, tokens:, :] = both


def local_rows(codes):
    owner = lax.axis_index("dp")
    scale = jnp.float32(1.0)
    for bit in range(4):
        scale = scale * jnp.where((owner >> bit) & 1 == 1, 0.25 ** (2**bit), 1.0)
    moved = codes.astype(f32) * scale
    row = jnp.where(moved < 256.0, moved - 128.0, moved * 0.5)
    return jnp.where((moved >= 128.0) & (moved < 512.0), row, -1.0)


def slot_kernel(recv_ref, values_ref, out_ref):
    sources, slots, tokens = out_ref.shape
    val_rows = values_ref.shape[0]

    def one(at, carry):
        grads = recv_ref[at, :tokens, :]
        scores = lax.dot_general(
            values_ref[...], grads, (((1,), (1,)), ((), ())), preferred_element_type=f32
        )
        row = local_rows(recv_ref[at, tokens:, :tokens]).astype(jnp.int32)
        high = row >> 3
        low = row & 7
        for part in range(slots // 8):
            mine = slice(part * 8, part * 8 + 8)
            low_now, high_now = low[mine], high[mine]
            acc = jnp.zeros((8, tokens), f32)
            for tile in range(val_rows // 8):
                got = jnp.take_along_axis(scores[tile * 8 : tile * 8 + 8], low_now, axis=0)
                acc = jnp.where(high_now == tile, got, acc)
            out_ref[at, mine, :] = acc
        return carry

    lax.fori_loop(0, sources, one, 0)


def value_kernel(first, recv_ref, *refs):
    carried, (out_ref, rows_ref, wide_ref, bag_ref, grads_ref) = refs[:-5], refs[-5:]
    val_rows = out_ref.shape[0]
    slots, tokens = rows_ref.shape
    sources = grads_ref.shape[0] // tokens
    iota = lax.broadcasted_iota(jnp.int32, (128, tokens), 0).astype(f32)

    def one(at, carry):
        span = pl.ds(pl.multiple_of(at * tokens, tokens), tokens)
        rows_ref[...] = local_rows(recv_ref[first + at, tokens:, :tokens])
        wide_ref[...] = recv_ref[first + at, tokens:, tokens:].astype(f32)
        grads_ref[span, :] = recv_ref[first + at, :tokens, :]
        for block in range(0, val_rows, 128):
            acc = jnp.zeros((128, tokens), f32)
            ids = iota + float(block)
            for slot in range(slots):
                hit = ids == rows_ref[slot : slot + 1, :]
                acc = jnp.where(hit, wide_ref[slot : slot + 1, :], acc)
            bag_ref[block : block + 128, span] = acc.astype(bf16)
        return carry

    lax.fori_loop(0, sources, one, 0)
    total = jnp.dot(bag_ref[...], grads_ref[...], preferred_element_type=f32)
    for ref in carried:
        total = total + ref[...]
    out_ref[...] = total


def part_kernel(
    slot_ref,
    weights_ref,
    picks_ref,
    queries_ref,
    keys_ref,
    layer_ref,
    out_ref,
    score_ref,
    sub_ref,
    mine_ref,
    sem,
):
    slots, tokens = slot_ref.shape
    halves, subs, width = keys_ref.shape
    quarter = lax.axis_index("mem") & 3
    cut = mine_ref.shape[1]
    fetch = pltpu.make_async_copy(
        queries_ref.at[:, pl.ds(pl.multiple_of(quarter * cut, cut), cut)], mine_ref, sem
    )
    fetch.start()
    weights = weights_ref[...]
    slot_grad = slot_ref[...]
    centered = slot_grad - jnp.sum(weights * slot_grad, axis=0, keepdims=True)
    score_ref[...] = weights * centered
    block = 64
    iota = lax.broadcasted_iota(jnp.int32, (block, tokens), 0)
    for half in range(halves):

        def one(at, carry, half=half):
            start = pl.multiple_of(at * block, block)
            ids = iota + start
            acc = jnp.zeros((block, tokens), f32)
            for slot in range(slots):
                hit = ids == picks_ref[half, slot : slot + 1, :]
                acc = acc + jnp.where(hit, score_ref[slot : slot + 1, :], 0.0)
            sub_ref[half, pl.ds(start, block), :] = acc.astype(bf16)
            return carry

        lax.fori_loop(0, subs // block, one, 0)
    dests = out_ref.shape[0]
    own = subs // dests
    layer = layer_ref[...]
    for half in range(halves):
        dquery = lax.dot_general(
            sub_ref[half], keys_ref[half], (((0,), (0,)), ((), ())), preferred_element_type=f32
        ).astype(bf16)
        proj = lax.dot_general(
            dquery, layer, (((0,), (0,)), ((), ())), preferred_element_type=f32
        ).astype(bf16)
        per = width // own
        for at in range(per):
            out_ref[half * per + at, :own, :] = proj[at * own : at * own + own]
    fetch.wait()
    key = jnp.dot(sub_ref[quarter >> 1], mine_ref[...], preferred_element_type=f32).astype(bf16)
    for at in range(dests):
        out_ref[at, own:, :] = key[at * own : at * own + own]


def sum_kernel(first, parts_ref, out_ref):
    rows = slice(first, first + out_ref.shape[0])
    total = parts_ref[0, rows, :].astype(f32)
    for at in range(1, parts_ref.shape[0]):
        total = total + parts_ref[at, rows, :].astype(f32)
    out_ref[...] = total


def join_kernel(own_ref, one_ref, two_ref, three_ref, out_ref):
    quarter = lax.axis_index("mem") & 3
    cut = own_ref.shape[1]
    for at, ref in enumerate((own_ref, one_ref, two_ref, three_ref)):
        there = quarter ^ at
        out_ref[there >> 1, :, pl.ds(pl.multiple_of((there & 1) * cut, cut), cut)] = ref[...]


def swap(x, mask, count):
    return lax.ppermute(x, "mem", [(at, at ^ mask) for at in range(count)])


def body(grad_out, values, slot_rows, weights, sub_picks, queries, sub_keys, layer_input):
    groups = lax.axis_size("dp")
    mem_count = lax.axis_size("mem")
    tokens, width = grad_out.shape
    slots = slot_rows.shape[1]
    val_rows = values.shape[0]
    halves, subs, key_width = sub_keys.shape
    weights_t = weights.T
    rows_t = slot_rows.T
    picks_t = jnp.swapaxes(sub_picks, 1, 2)

    sent = run(
        pack_kernel, shape((groups, tokens + slots, width), bf16), (grad_out, rows_t, weights_t)
    )
    recv = lax.all_to_all(sent, "dp", 0, 0, tiled=True)
    slot_parts = run(slot_kernel, shape((groups, slots, tokens), f32), (recv, values))
    slot_parts = lax.all_to_all(slot_parts, "dp", 0, 0, tiled=True)
    slot_grad = jnp.sum(slot_parts, axis=0)

    def value_part(first, count, args):
        return run(
            functools.partial(value_kernel, first),
            shape((val_rows, width), f32),
            args,
            scratch=(
                pltpu.VMEM((slots, tokens), f32),
                pltpu.VMEM((slots, tokens), f32),
                pltpu.VMEM((val_rows, count * tokens), bf16),
                pltpu.VMEM((count * tokens, width), bf16),
            ),
            flops=2 * 10**9,
            data=2**20,
        )

    half = groups // 2
    slot_grad = slot_grad + swap(slot_grad, 1, mem_count)
    slot_grad, recv = lax.optimization_barrier((slot_grad, recv))
    value_grad = value_part(0, half, (recv,))
    slot_grad = slot_grad + swap(slot_grad, 2, mem_count)
    slot_grad, value_grad = lax.optimization_barrier((slot_grad, value_grad))
    value_grad = value_part(half, groups - half, (recv, value_grad))
    slot_grad = slot_grad + swap(slot_grad, 4, mem_count)
    slot_grad, value_grad = lax.optimization_barrier((slot_grad, value_grad))
    slot_grad = slot_grad + swap(slot_grad, 12, mem_count)

    own = subs // groups
    parts = run(
        part_kernel,
        shape((groups, 2 * own, width), bf16),
        (slot_grad, weights_t, picks_t, queries, sub_keys, layer_input),
        scratch=(
            pltpu.VMEM((slots, tokens), f32),
            pltpu.VMEM((halves, subs, tokens), bf16),
            pltpu.VMEM((tokens, queries.shape[1] // 4), bf16),
            pltpu.SemaphoreType.DMA(()),
        ),
        far=(3,),
    )
    parts = lax.all_to_all(parts, "dp", 0, 0, tiled=True)
    key = run(functools.partial(sum_kernel, own), shape((own, width), f32), (parts,))
    others = [swap(key, mask, mem_count) for mask in (1, 2, 3)]
    proj_grad = run(
        functools.partial(sum_kernel, 0),
        shape((own, width), f32),
        (parts,),
        flops=10**9,
        data=2**19,
    )
    key_grad = run(join_kernel, shape((halves, own, key_width), f32), (key, *others))
    return (value_grad, key_grad, proj_grad)


def solution(mesh):
    return jax.shard_map(
        body,
        mesh=mesh,
        in_specs=(
            P("dp", "mem"),
            P("dp", "mem"),
            P("dp", None),
            P("dp", None),
            P(None, "dp", None),
            P("dp", None),
            P(),
            P("dp", "mem"),
        ),
        out_specs=(P("dp", "mem"), P(None, "dp", None), P("dp", "mem")),
        check_vma=False,
    )
```

```python
import functools

import jax
import jax.numpy as jnp
from jax import lax
from jax.experimental import pallas as pl
from jax.experimental.pallas import tpu as pltpu
from jax.sharding import PartitionSpec as P


f32 = jnp.float32
bf16 = jnp.bfloat16
VM = pl.BlockSpec(memory_space=pltpu.VMEM)
FAR = pl.BlockSpec(memory_space=pltpu.HBM)


def run(kernel, outs, args, scratch=(), flops=0, data=0, far=(), room=16):
    return pl.pallas_call(
        kernel,
        out_shape=outs,
        in_specs=[FAR if at in far else VM for at in range(len(args))],
        out_specs=jax.tree.map(lambda _: VM, outs),
        scratch_shapes=list(scratch),
        cost_estimate=pl.CostEstimate(flops=flops, bytes_accessed=data, transcendentals=0),
        compiler_params=pltpu.CompilerParams(vmem_limit_bytes=room * 2**20),
    )(*args)


def shape(dims, dtype):
    return jax.ShapeDtypeStruct(dims, dtype)


def pack_kernel(grad_ref, rows_ref, weights_ref, out_ref, ids_ref, wide_ref, sems):
    tokens = grad_ref.shape[0]
    copies = (
        pltpu.make_async_copy(rows_ref, ids_ref, sems.at[0]),
        pltpu.make_async_copy(weights_ref, wide_ref, sems.at[1]),
        pltpu.make_async_copy(grad_ref, out_ref.at[pl.ds(0, tokens), :], sems.at[2]),
    )
    for copy in copies:
        copy.start()
    copies[0].wait()
    copies[1].wait()
    ids = ids_ref[...]
    power = ids >> 7
    scale = (1 << (power & 15)).astype(f32) * jnp.where(power >= 16, 65536.0, 1.0)
    codes = ((ids & 127) + 128).astype(f32) * scale
    out_ref[tokens:, :] = jnp.concatenate([codes, wide_ref[...]], axis=1).astype(bf16)
    copies[2].wait()


def local_rows(codes):
    owner = lax.axis_index("dp")
    scale = jnp.float32(1.0)
    for bit in range(4):
        scale = scale * jnp.where((owner >> bit) & 1 == 1, 0.25 ** (2**bit), 1.0)
    moved = codes.astype(f32) * scale
    row = jnp.where(moved < 256.0, moved - 128.0, moved * 0.5)
    return jnp.where((moved >= 128.0) & (moved < 512.0), row, -1.0)


def one_slot_block(block_ref, values_ref, out_ref):
    slots, tokens = out_ref.shape
    val_rows = values_ref.shape[0]
    scores = lax.dot_general(
        values_ref[...],
        block_ref[:tokens, :],
        (((1,), (1,)), ((), ())),
        preferred_element_type=f32,
    )
    row = local_rows(block_ref[tokens:, :tokens]).astype(jnp.int32)
    high = row >> 3
    low = row & 7
    for part in range(slots // 8):
        mine = slice(part * 8, part * 8 + 8)
        low_now, high_now = low[mine], high[mine]
        acc = jnp.zeros((8, tokens), f32)
        for tile in range(val_rows // 8):
            got = jnp.take_along_axis(scores[tile * 8 : tile * 8 + 8], low_now, axis=0)
            acc = jnp.where(high_now == tile, got, acc)
        out_ref[mine, :] = acc


def slot_kernel(recv_ref, values_ref, out_ref):
    def one(at, carry):
        one_slot_block(recv_ref.at[at], values_ref, out_ref.at[at])
        return carry

    lax.fori_loop(0, recv_ref.shape[0], one, 0)


def last_slot_kernel(side, order, recv_ref, values_ref, *refs):
    done, out_ref = refs[:-1], refs[-1]
    owner = lax.axis_index("dp")
    row, column = owner // side, owner % side

    def place(group, at):
        return ((row + side - order[group]) % side) * side + (column + side - order[at]) % side

    for at in range(side):
        one_slot_block(recv_ref.at[at], values_ref, out_ref.at[place(side - 1, at)])
    for group, ref in enumerate(done):
        for at in range(side):
            out_ref[place(group, at)] = ref[at]


def value_kernel(count, *refs):
    groups, carried = refs[:count], refs[count:-5]
    out_ref, rows_ref, wide_ref, bag_ref, grads_ref = refs[-5:]
    val_rows = out_ref.shape[0]
    slots, tokens = rows_ref.shape
    iota = lax.broadcasted_iota(jnp.int32, (128, tokens), 0).astype(f32)
    for place, recv_ref in enumerate(groups):
        sources = recv_ref.shape[0]

        def one(at, carry, recv_ref=recv_ref, first=place * sources):
            span = pl.ds(pl.multiple_of((first + at) * tokens, tokens), tokens)
            rows_ref[...] = local_rows(recv_ref[at, tokens:, :tokens])
            wide_ref[...] = recv_ref[at, tokens:, tokens:].astype(f32)
            grads_ref[span, :] = recv_ref[at, :tokens, :]
            for block in range(0, val_rows, 128):
                acc = jnp.zeros((128, tokens), f32)
                ids = iota + float(block)
                for slot in range(slots):
                    hit = ids == rows_ref[slot : slot + 1, :]
                    acc = jnp.where(hit, wide_ref[slot : slot + 1, :], acc)
                bag_ref[block : block + 128, span] = acc.astype(bf16)
            return carry

        lax.fori_loop(0, sources, one, 0)
    total = jnp.dot(bag_ref[...], grads_ref[...], preferred_element_type=f32)
    for ref in carried:
        total = total + ref[...]
    out_ref[...] = total


def part_kernel(
    slot_ref,
    weights_ref,
    picks_ref,
    queries_ref,
    keys_ref,
    layer_ref,
    out_ref,
    score_ref,
    sub_ref,
    dquery_ref,
    mine_ref,
    sem,
):
    slots, tokens = score_ref.shape
    halves, subs, width = keys_ref.shape
    block = sub_ref.shape[1]
    per_half = subs // block
    quarter = lax.axis_index("mem") & 3
    cut = mine_ref.shape[1]
    fetch = pltpu.make_async_copy(
        queries_ref.at[:, pl.ds(pl.multiple_of(quarter * cut, cut), cut)], mine_ref, sem
    )
    fetch.start()
    weights = weights_ref[...]
    slot_grad = slot_ref[0]
    for at in range(1, slot_ref.shape[0]):
        slot_grad = slot_grad + slot_ref[at]
    centered = slot_grad - jnp.sum(weights * slot_grad, axis=0, keepdims=True)
    score_ref[...] = weights * centered
    dquery_ref[...] = jnp.zeros_like(dquery_ref)
    piece = 64
    iota = lax.broadcasted_iota(jnp.int32, (piece, tokens), 0)

    def build(step):
        half = step // per_half
        start = (step % per_half) * block
        for part in range(0, block, piece):
            ids = iota + (start + part)
            acc = jnp.zeros((piece, tokens), f32)
            for slot in range(slots):
                hit = ids == picks_ref[half, slot : slot + 1, :]
                acc = acc + jnp.where(hit, score_ref[slot : slot + 1, :], 0.0)
            sub_ref[step, part : part + piece, :] = acc.astype(bf16)

    def multiply(step):
        half = step // per_half
        start = pl.multiple_of((step % per_half) * block, block)
        dquery_ref[half] = dquery_ref[half] + lax.dot_general(
            sub_ref[step],
            keys_ref[half, pl.ds(start, block), :],
            (((0,), (0,)), ((), ())),
            preferred_element_type=f32,
        )

    def one(step, carry):
        build(step)
        multiply(step - 1)
        return carry

    steps = halves * per_half
    build(0)
    lax.fori_loop(1, steps, one, 0)
    multiply(steps - 1)
    dests = out_ref.shape[0]
    own = subs // dests
    layer = layer_ref[...]
    for half in range(halves):
        proj = lax.dot_general(
            dquery_ref[half].astype(bf16), layer, (((0,), (0,)), ((), ())), preferred_element_type=f32
        ).astype(bf16)
        per = width // own
        for at in range(per):
            out_ref[half * per + at, :own, :] = proj[at * own : at * own + own]
    fetch.wait()
    per = block // own
    for step in range(per_half):
        key = jnp.dot(
            sub_ref[(quarter >> 1) * per_half + step], mine_ref[...], preferred_element_type=f32
        ).astype(bf16)
        for at in range(per):
            out_ref[step * per + at, own:, :] = key[at * own : at * own + own]


def sum_kernel(first, parts_ref, out_ref):
    rows = slice(first, first + out_ref.shape[0])
    total = parts_ref[0, rows, :].astype(f32)
    for at in range(1, parts_ref.shape[0]):
        total = total + parts_ref[at, rows, :].astype(f32)
    out_ref[...] = total.astype(out_ref.dtype)


def join_kernel(own_ref, one_ref, two_ref, three_ref, out_ref):
    quarter = lax.axis_index("mem") & 3
    cut = own_ref.shape[1]
    for at, ref in enumerate((own_ref, one_ref, two_ref, three_ref)):
        there = quarter ^ at
        out_ref[there >> 1, :, pl.ds(pl.multiple_of((there & 1) * cut, cut), cut)] = ref[...].astype(f32)


def swap(x, mask, count):
    return lax.ppermute(x, "mem", [(at, at ^ mask) for at in range(count)])


def body(grad_out, values, slot_rows, weights, sub_picks, queries, sub_keys, layer_input):
    groups = lax.axis_size("dp")
    mem_count = lax.axis_size("mem")
    tokens, width = grad_out.shape
    slots = slot_rows.shape[1]
    val_rows = values.shape[0]
    halves, subs, key_width = sub_keys.shape
    weights_t = weights.T
    rows_t = slot_rows.T
    picks_t = jnp.swapaxes(sub_picks, 1, 2)

    sent = run(
        pack_kernel,
        shape((tokens + slots, width), bf16),
        (grad_out, rows_t, weights_t),
        scratch=(
            pltpu.VMEM((slots, tokens), jnp.int32),
            pltpu.VMEM((slots, tokens), f32),
            pltpu.SemaphoreType.DMA((3,)),
        ),
        far=(0, 1, 2),
        room=60,
    )

    side = 4
    order = (0, 2, 3, 1)

    def along_x(x, shift):
        return lax.ppermute(
            x, "dp", [(at, at // side * side + (at + shift) % side) for at in range(groups)]
        )

    def along_y(x, shift):
        return lax.ppermute(x, "dp", [(at, (at + shift * side) % groups) for at in range(groups)])

    near = jnp.stack([sent] + [along_x(sent, shift) for shift in order[1:]])
    recv = [near] + [along_y(near, shift) for shift in order[1:]]

    def slot_part(group):
        return run(
            slot_kernel,
            shape((side, slots, tokens), f32),
            (group, values),
            flops=10**9,
            data=2**19,
        )

    def value_part(members, carried):
        count = len(members) * side * tokens
        return run(
            functools.partial(value_kernel, len(members)),
            shape((val_rows, width), f32),
            (*members, *carried),
            scratch=(
                pltpu.VMEM((slots, tokens), f32),
                pltpu.VMEM((slots, tokens), f32),
                pltpu.VMEM((val_rows, count), bf16),
                pltpu.VMEM((count, width), bf16),
            ),
            flops=10**9 * len(members),
            data=2**19 * len(members),
        )

    slot_parts = [slot_part(group) for group in recv[:-1]]
    value_grad = value_part(recv, ())
    slot_parts = run(
        functools.partial(last_slot_kernel, side, order),
        shape((groups, slots, tokens), f32),
        (recv[-1], values, *slot_parts),
    )
    slot_parts = lax.all_to_all(slot_parts, "dp", 0, 0, tiled=True)
    slot_grad = jnp.sum(slot_parts, axis=0)
    slot_grad = jnp.broadcast_to(slot_grad, (mem_count, slots, tokens))
    slot_grad = lax.all_to_all(slot_grad, "mem", 0, 0, tiled=True)

    own = subs // groups
    parts = run(
        part_kernel,
        shape((groups, 2 * own, width), bf16),
        (slot_grad, weights_t, picks_t, queries, sub_keys, layer_input),
        scratch=(
            pltpu.VMEM((slots, tokens), f32),
            pltpu.VMEM((halves * 4, subs // 4, tokens), bf16),
            pltpu.VMEM((halves, tokens, key_width), f32),
            pltpu.VMEM((tokens, queries.shape[1] // 4), bf16),
            pltpu.SemaphoreType.DMA(()),
        ),
        far=(3,),
    )
    parts = lax.all_to_all(parts, "dp", 0, 0, tiled=True)
    key = run(functools.partial(sum_kernel, own), shape((own, width), bf16), (parts,))
    others = [swap(key, mask, mem_count) for mask in (1, 2, 3)]
    proj_grad = run(
        functools.partial(sum_kernel, 0),
        shape((own, width), f32),
        (parts,),
        flops=10**9,
        data=2**19,
    )
    key_grad = run(join_kernel, shape((halves, own, key_width), f32), (key, *others))
    return (value_grad, key_grad, proj_grad)


def solution(mesh):
    return jax.shard_map(
        body,
        mesh=mesh,
        in_specs=(
            P("dp", "mem"),
            P("dp", "mem"),
            P("dp", None),
            P("dp", None),
            P(None, "dp", None),
            P("dp", None),
            P(),
            P("dp", "mem"),
        ),
        out_specs=(P("dp", "mem"), P(None, "dp", None), P("dp", "mem")),
        check_vma=False,
    )
```

```python
import functools

import jax
import jax.numpy as jnp
from jax import lax
from jax.experimental import pallas as pl
from jax.experimental.pallas import tpu as pltpu
from jax.sharding import PartitionSpec as P


f32 = jnp.float32
bf16 = jnp.bfloat16
VM = pl.BlockSpec(memory_space=pltpu.VMEM)
FAR = pl.BlockSpec(memory_space=pltpu.HBM)


def run(kernel, outs, args, scratch=(), flops=0, data=0, far=(), out_spec=VM, room=16):
    return pl.pallas_call(
        kernel,
        out_shape=outs,
        in_specs=[FAR if at in far else VM for at in range(len(args))],
        out_specs=jax.tree.map(lambda _: out_spec, outs),
        scratch_shapes=list(scratch),
        cost_estimate=pl.CostEstimate(flops=flops, bytes_accessed=data, transcendentals=0),
        compiler_params=pltpu.CompilerParams(vmem_limit_bytes=room * 2**20),
    )(*args)


def shape(dims, dtype):
    return jax.ShapeDtypeStruct(dims, dtype)


def row_codes(ids):
    power = ids >> 7
    scale = (1 << (power & 15)).astype(f32) * jnp.where(power >= 16, 65536.0, 1.0)
    return ((ids & 127) + 128).astype(f32) * scale


def pack_kernel(grad_ref, rows_ref, weights_ref, out_ref, one_ref, ids_ref, wide_ref, in_sem, out_sem):
    tokens = grad_ref.shape[0]
    copies = (
        pltpu.make_async_copy(rows_ref, ids_ref, in_sem.at[0]),
        pltpu.make_async_copy(weights_ref, wide_ref, in_sem.at[1]),
        pltpu.make_async_copy(grad_ref, one_ref.at[pl.ds(0, tokens), :], in_sem.at[2]),
    )
    for copy in copies:
        copy.start()
    copies[0].wait()
    copies[1].wait()
    both = jnp.concatenate([row_codes(ids_ref[...]), wide_ref[...]], axis=1)
    one_ref[tokens:, :] = both.astype(bf16)
    copies[2].wait()
    sends = [
        pltpu.make_async_copy(one_ref, out_ref.at[at], out_sem.at[at])
        for at in range(out_ref.shape[0])
    ]
    for send in sends:
        send.start()
    for send in sends:
        send.wait()


def owner_scale(base):
    owner = lax.axis_index("dp")
    scale = jnp.float32(1.0)
    for bit in range(4):
        scale = scale * jnp.where((owner >> bit) & 1 == 1, base ** (2 ** (bit + 1)), 1.0)
    return scale


def local_rows(codes):
    moved = codes.astype(f32) * owner_scale(0.5)
    row = jnp.where(moved < 256.0, moved - 128.0, moved * 0.5)
    return jnp.where((moved >= 128.0) & (moved < 512.0), row, -1.0)


def slot_kernel(recv_ref, values_ref, out_ref):
    sources, slots, tokens = out_ref.shape
    val_rows = values_ref.shape[0]
    together = 4

    def one(step, carry):
        blocks = [step * together + at for at in range(together)]
        scores = [
            lax.dot_general(
                values_ref[...],
                recv_ref[at, :tokens, :],
                (((1,), (1,)), ((), ())),
                preferred_element_type=f32,
            )
            for at in blocks
        ]
        for at, score in zip(blocks, scores):
            row = local_rows(recv_ref[at, tokens:, :tokens]).astype(jnp.int32)
            high = row >> 3
            low = row & 7
            for part in range(slots // 8):
                mine = slice(part * 8, part * 8 + 8)
                low_now, high_now = low[mine], high[mine]
                acc = jnp.zeros((8, tokens), f32)
                for tile in range(val_rows // 8):
                    got = jnp.take_along_axis(score[tile * 8 : tile * 8 + 8], low_now, axis=0)
                    acc = jnp.where(high_now == tile, got, acc)
                out_ref[at, mine, :] = acc
        return carry

    lax.fori_loop(0, sources // together, one, 0)


def wide_row(ref, at):
    return jnp.broadcast_to(ref[at, :][None, :], (16, ref.shape[1])).astype(bf16)


def value_kernel(first, recv_ref, *refs):
    carried, (out_ref, rows_ref, wide_ref, bag_ref, grads_ref) = refs[:-5], refs[-5:]
    val_rows = out_ref.shape[0]
    slots, tokens = rows_ref.shape
    sources = grads_ref.shape[0] // tokens
    tiles = val_rows // 16
    ids = lax.broadcasted_iota(jnp.int32, (val_rows, tokens), 0)
    codes = (row_codes(ids) * owner_scale(2.0)).astype(bf16)
    codes = [codes[tile * 16 : tile * 16 + 16] for tile in range(tiles)]

    def one(at, carry):
        span = pl.ds(pl.multiple_of(at * tokens, tokens), tokens)
        rows_ref[...] = recv_ref[first + at, tokens:, :tokens].astype(f32)
        wide_ref[...] = recv_ref[first + at, tokens:, tokens:].astype(f32)
        grads_ref[span, :] = recv_ref[first + at, :tokens, :]
        bags = [jnp.zeros((16, tokens), bf16)] * tiles
        for slot in range(slots):
            row, weight = wide_row(rows_ref, slot), wide_row(wide_ref, slot)
            bags = [jnp.where(code == row, weight, bag) for code, bag in zip(codes, bags)]
        for tile in range(tiles):
            bag_ref[tile * 16 : tile * 16 + 16, span] = bags[tile]
        return carry

    lax.fori_loop(0, sources, one, 0)
    total = jnp.dot(bag_ref[...], grads_ref[...], preferred_element_type=f32)
    for ref in carried:
        total = total + ref[...]
    out_ref[...] = total


def part_kernel(
    slot_ref,
    weights_ref,
    picks_ref,
    queries_ref,
    keys_ref,
    layer_ref,
    out_ref,
    score_ref,
    pick_code_ref,
    pick_wide_ref,
    score_wide_ref,
    sub_ref,
    mine_ref,
    sem,
):
    slots, tokens = slot_ref.shape
    halves, subs, width = keys_ref.shape
    quarter = lax.axis_index("mem") & 3
    cut = mine_ref.shape[1]
    fetch = pltpu.make_async_copy(
        queries_ref.at[:, pl.ds(pl.multiple_of(quarter * cut, cut), cut)], mine_ref, sem
    )
    fetch.start()
    weights = weights_ref[...]
    slot_grad = slot_ref[...]
    centered = slot_grad - jnp.sum(weights * slot_grad, axis=0, keepdims=True)
    score_ref[0] = weights * centered
    block = 128
    tiles = block // 16
    base = lax.broadcasted_iota(jnp.int32, (block, tokens), 0).astype(f32) + 128.0
    for half in range(halves):
        picks = picks_ref[half]
        merged = jnp.zeros((slots, tokens), f32)
        for slot in range(slots):
            same = picks == picks_ref[half, slot : slot + 1, :]
            merged = merged + jnp.where(same, score_ref[0, slot : slot + 1, :], 0.0)
        score_ref[1] = merged
        pick_code_ref[...] = row_codes(picks)
        for slot in range(slots):
            pick_wide_ref[slot] = wide_row(pick_code_ref, slot)
            score_wide_ref[slot] = wide_row(score_ref.at[1], slot)

        def one(at, carry, half=half):
            codes = (base * (1 << at).astype(f32)).astype(bf16)
            codes = [codes[tile * 16 : tile * 16 + 16] for tile in range(tiles)]
            accs = [jnp.zeros((16, tokens), bf16)] * tiles
            for slot in range(slots):
                pick, score = pick_wide_ref[slot], score_wide_ref[slot]
                accs = [jnp.where(code == pick, score, acc) for code, acc in zip(codes, accs)]
            for tile in range(tiles):
                start = pl.multiple_of(at * block + tile * 16, 16)
                sub_ref[half, pl.ds(start, 16), :] = accs[tile]
            return carry

        lax.fori_loop(0, subs // block, one, 0)
    dests = out_ref.shape[0]
    own = subs // dests
    layer = layer_ref[...]
    for half in range(halves):
        dquery = lax.dot_general(
            sub_ref[half], keys_ref[half], (((0,), (0,)), ((), ())), preferred_element_type=f32
        ).astype(bf16)
        proj = lax.dot_general(
            dquery, layer, (((0,), (0,)), ((), ())), preferred_element_type=f32
        ).astype(bf16)
        per = width // own
        for at in range(per):
            out_ref[half * per + at, :own, :] = proj[at * own : at * own + own]
    fetch.wait()
    key = jnp.dot(sub_ref[quarter >> 1], mine_ref[...], preferred_element_type=f32).astype(bf16)
    for at in range(dests):
        out_ref[at, own:, :] = key[at * own : at * own + own]


def sum_kernel(first, parts_ref, out_ref):
    rows = slice(first, first + out_ref.shape[0])
    total = parts_ref[0, rows, :].astype(f32)
    for at in range(1, parts_ref.shape[0]):
        total = total + parts_ref[at, rows, :].astype(f32)
    out_ref[...] = total.astype(out_ref.dtype)


def join_kernel(own_ref, one_ref, two_ref, three_ref, out_ref):
    quarter = lax.axis_index("mem") & 3
    cut = own_ref.shape[1]
    for at, ref in enumerate((own_ref, one_ref, two_ref, three_ref)):
        there = quarter ^ at
        out_ref[there >> 1, :, pl.ds(pl.multiple_of((there & 1) * cut, cut), cut)] = ref[...].astype(f32)


def swap(x, mask, count):
    return lax.ppermute(x, "mem", [(at, at ^ mask) for at in range(count)])


def body(grad_out, values, slot_rows, weights, sub_picks, queries, sub_keys, layer_input):
    groups = lax.axis_size("dp")
    mem_count = lax.axis_size("mem")
    tokens, width = grad_out.shape
    slots = slot_rows.shape[1]
    val_rows = values.shape[0]
    halves, subs, key_width = sub_keys.shape
    weights_t = weights.T
    rows_t = slot_rows.T
    picks_t = jnp.swapaxes(sub_picks, 1, 2)

    sent = run(
        pack_kernel,
        shape((groups, tokens + slots, width), bf16),
        (grad_out, rows_t, weights_t),
        scratch=(
            pltpu.VMEM((tokens + slots, width), bf16),
            pltpu.VMEM((slots, tokens), jnp.int32),
            pltpu.VMEM((slots, tokens), f32),
            pltpu.SemaphoreType.DMA((3,)),
            pltpu.SemaphoreType.DMA((groups,)),
        ),
        far=(0, 1, 2),
        out_spec=FAR,
        room=60,
    )
    recv = lax.all_to_all(sent, "dp", 0, 0, tiled=True)
    slot_parts = run(slot_kernel, shape((groups, slots, tokens), f32), (recv, values))
    slot_parts = lax.all_to_all(slot_parts, "dp", 0, 0, tiled=True)
    slot_grad = jnp.sum(slot_parts, axis=0)

    def value_part(first, count, args):
        return run(
            functools.partial(value_kernel, first),
            shape((val_rows, width), f32),
            args,
            scratch=(
                pltpu.VMEM((slots, tokens), f32),
                pltpu.VMEM((slots, tokens), f32),
                pltpu.VMEM((val_rows, count * tokens), bf16),
                pltpu.VMEM((count * tokens, width), bf16),
            ),
            flops=2 * 10**9,
            data=2**20,
        )

    half = groups // 2
    one, two, three = (swap(slot_grad, mask, mem_count) for mask in (1, 2, 3))
    slot_grad = (slot_grad + one) + (two + three)
    slot_grad, recv = lax.optimization_barrier((slot_grad, recv))
    value_grad = value_part(0, half, (recv,))
    slot_grad = slot_grad + swap(slot_grad, 4, mem_count)
    slot_grad, value_grad = lax.optimization_barrier((slot_grad, value_grad))
    value_grad = value_part(half, groups - half, (recv, value_grad))
    slot_grad = slot_grad + swap(slot_grad, 12, mem_count)
    slot_grad, value_grad = lax.optimization_barrier((slot_grad, value_grad))

    own = subs // groups
    parts = run(
        part_kernel,
        shape((groups, 2 * own, width), bf16),
        (slot_grad, weights_t, picks_t, queries, sub_keys, layer_input),
        scratch=(
            pltpu.VMEM((2, slots, tokens), f32),
            pltpu.VMEM((slots, tokens), f32),
            pltpu.VMEM((slots, 16, tokens), bf16),
            pltpu.VMEM((slots, 16, tokens), bf16),
            pltpu.VMEM((halves, subs, tokens), bf16),
            pltpu.VMEM((tokens, queries.shape[1] // 4), bf16),
            pltpu.SemaphoreType.DMA(()),
        ),
        far=(3,),
    )
    parts = lax.all_to_all(parts, "dp", 0, 0, tiled=True)
    key = run(functools.partial(sum_kernel, own), shape((own, width), bf16), (parts,))
    others = [swap(key, mask, mem_count) for mask in (1, 2, 3)]
    proj_grad = run(
        functools.partial(sum_kernel, 0),
        shape((own, width), f32),
        (parts,),
        flops=10**9,
        data=2**19,
    )
    key_grad = run(join_kernel, shape((halves, own, key_width), f32), (key, *others))
    return (value_grad, key_grad, proj_grad)


def solution(mesh):
    return jax.shard_map(
        body,
        mesh=mesh,
        in_specs=(
            P("dp", "mem"),
            P("dp", "mem"),
            P("dp", None),
            P("dp", None),
            P(None, "dp", None),
            P("dp", None),
            P(),
            P("dp", "mem"),
        ),
        out_specs=(P("dp", "mem"), P(None, "dp", None), P("dp", "mem")),
        check_vma=False,
    )
```

```python
import functools

import jax
import jax.numpy as jnp
from jax import lax
from jax.experimental import pallas as pl
from jax.experimental.pallas import tpu as pltpu
from jax.sharding import PartitionSpec as P


f32 = jnp.float32
bf16 = jnp.bfloat16
SIDE = 4
VM = pl.BlockSpec(memory_space=pltpu.VMEM)
FAR = pl.BlockSpec(memory_space=pltpu.HBM)


def run(kernel, outs, args, scratch=(), flops=0, data=0, far=(), out_spec=VM, room=16):
    return pl.pallas_call(
        kernel,
        out_shape=outs,
        in_specs=[FAR if at in far else VM for at in range(len(args))],
        out_specs=jax.tree.map(lambda _: out_spec, outs),
        scratch_shapes=list(scratch),
        cost_estimate=pl.CostEstimate(flops=flops, bytes_accessed=data, transcendentals=0),
        compiler_params=pltpu.CompilerParams(vmem_limit_bytes=room * 2**20),
    )(*args)


def shape(dims, dtype):
    return jax.ShapeDtypeStruct(dims, dtype)


def row_codes(ids):
    power = ids >> 7
    scale = (1 << (power & 15)).astype(f32) * jnp.where(power >= 16, 65536.0, 1.0)
    return ((ids & 127) + 128).astype(f32) * scale


def pack_kernel(grad_ref, rows_ref, weights_ref, out_ref, one_ref, ids_ref, wide_ref, in_sem, out_sem):
    tokens = grad_ref.shape[0]
    copies = (
        pltpu.make_async_copy(rows_ref, ids_ref, in_sem.at[0]),
        pltpu.make_async_copy(weights_ref, wide_ref, in_sem.at[1]),
        pltpu.make_async_copy(grad_ref, one_ref.at[pl.ds(0, tokens), :], in_sem.at[2]),
    )
    for copy in copies:
        copy.start()
    copies[0].wait()
    copies[1].wait()
    both = jnp.concatenate([row_codes(ids_ref[...]), wide_ref[...]], axis=1)
    one_ref[tokens:, :] = both.astype(bf16)
    copies[2].wait()
    sends = [
        pltpu.make_async_copy(one_ref, out_ref.at[at], out_sem.at[at])
        for at in range(out_ref.shape[0])
    ]
    for send in sends:
        send.start()
    for send in sends:
        send.wait()


def power_of(base, exponent, bits):
    scale = jnp.float32(1.0)
    for bit in range(bits):
        scale = scale * jnp.where((exponent >> bit) & 1 == 1, base ** (2**bit), 1.0)
    return scale


def group_rows(codes):
    row = lax.axis_index("dp") // SIDE
    moved = codes.astype(f32) * power_of(2.0**-8, row, 2)
    inside = (moved >= 128.0) & (moved < 32768.0)
    local = jnp.full(codes.shape, -128, jnp.int32)
    for step in (4, 2, 1):
        above = moved >= 128.0 * 2.0**step
        moved = jnp.where(above, moved * 2.0**-step, moved)
        local = jnp.where(above, local + 128 * step, local)
    return jnp.where(inside, local + moved.astype(jnp.int32), -1)


def slot_kernel(recv_ref, *refs):
    values_refs, out_ref = refs[:-1], refs[-1]
    blocks, slots, tokens = out_ref.shape
    val_rows = values_refs[0].shape[0]
    column = lax.axis_index("dp") % SIDE
    for at in range(blocks):
        row = group_rows(recv_ref[at, tokens:, :tokens])
        high = row >> 3
        low = row & 7
        accs = [jnp.zeros((8, tokens), f32) for _ in range(slots // 8)]
        for shift, values_ref in enumerate(values_refs):
            score = lax.dot_general(
                values_ref[...],
                recv_ref[at, :tokens, :],
                (((1,), (1,)), ((), ())),
                preferred_element_type=f32,
            )
            first = ((column + SIDE - shift) % SIDE) * (val_rows // 8)
            for part in range(slots // 8):
                mine = slice(part * 8, part * 8 + 8)
                low_now, high_now = low[mine], high[mine] - first
                for tile in range(val_rows // 8):
                    got = jnp.take_along_axis(score[tile * 8 : tile * 8 + 8], low_now, axis=0)
                    accs[part] = jnp.where(high_now == tile, got, accs[part])
        for part in range(slots // 8):
            out_ref[at, part * 8 : part * 8 + 8, :] = accs[part]


def wide_row(ref, at):
    return jnp.broadcast_to(ref[at, :][None, :], (16, ref.shape[1])).astype(bf16)


def value_kernel(shifts, recv_ref, *refs):
    out_refs, (rows_ref, wide_ref, bag_ref, grads_ref) = refs[:-4], refs[-4:]
    blocks = recv_ref.shape[0]
    val_rows = out_refs[0].shape[0]
    slots, tokens = rows_ref.shape[1:]
    tiles = val_rows // 16
    owner = lax.axis_index("dp")
    row, column = owner // SIDE, owner % SIDE
    base = row_codes(lax.broadcasted_iota(jnp.int32, (val_rows, tokens), 0))
    for at in range(blocks):
        rows_ref[at] = recv_ref[at, tokens:, :tokens].astype(f32)
        wide_ref[at] = recv_ref[at, tokens:, tokens:].astype(f32)
        grads_ref[at * tokens : at * tokens + tokens, :] = recv_ref[at, :tokens, :]
    for shift, out_ref in zip(shifts, out_refs):
        holder = row * SIDE + (column + shift) % SIDE
        codes = (base * power_of(4.0, holder, 4)).astype(bf16)
        codes = [codes[tile * 16 : tile * 16 + 16] for tile in range(tiles)]

        def one(at, carry, codes=codes):
            span = pl.ds(pl.multiple_of(at * tokens, tokens), tokens)
            bags = [jnp.zeros((16, tokens), bf16)] * tiles
            for slot in range(slots):
                code_now = wide_row(rows_ref.at[at], slot)
                weight = wide_row(wide_ref.at[at], slot)
                bags = [jnp.where(code == code_now, weight, bag) for code, bag in zip(codes, bags)]
            for tile in range(tiles):
                bag_ref[tile * 16 : tile * 16 + 16, span] = bags[tile]
            return carry

        lax.fori_loop(0, blocks, one, 0)
        total = jnp.dot(bag_ref[...], grads_ref[...], preferred_element_type=f32)
        out_ref[...] = total.astype(out_ref.dtype)


def add_kernel(*refs):
    total = refs[0][...].astype(f32)
    for ref in refs[1:-1]:
        total = total + ref[...].astype(f32)
    refs[-1][...] = total


def part_kernel(
    slot_ref,
    weights_ref,
    picks_ref,
    queries_ref,
    keys_ref,
    layer_ref,
    out_ref,
    score_ref,
    pick_code_ref,
    pick_wide_ref,
    score_wide_ref,
    sub_ref,
    mine_ref,
    sem,
):
    slots, tokens = slot_ref.shape
    halves, subs, width = keys_ref.shape
    quarter = lax.axis_index("mem") & 3
    cut = mine_ref.shape[1]
    fetch = pltpu.make_async_copy(
        queries_ref.at[:, pl.ds(pl.multiple_of(quarter * cut, cut), cut)], mine_ref, sem
    )
    fetch.start()
    weights = weights_ref[...]
    slot_grad = slot_ref[...]
    centered = slot_grad - jnp.sum(weights * slot_grad, axis=0, keepdims=True)
    score_ref[0] = weights * centered
    block = 128
    tiles = block // 16
    base = lax.broadcasted_iota(jnp.int32, (block, tokens), 0).astype(f32) + 128.0
    for half in range(halves):
        picks = picks_ref[half]
        merged = jnp.zeros((slots, tokens), f32)
        for slot in range(slots):
            same = picks == picks_ref[half, slot : slot + 1, :]
            merged = merged + jnp.where(same, score_ref[0, slot : slot + 1, :], 0.0)
        score_ref[1] = merged
        pick_code_ref[...] = row_codes(picks)
        for slot in range(slots):
            pick_wide_ref[slot] = wide_row(pick_code_ref, slot)
            score_wide_ref[slot] = wide_row(score_ref.at[1], slot)

        def one(at, carry, half=half):
            codes = (base * (1 << at).astype(f32)).astype(bf16)
            codes = [codes[tile * 16 : tile * 16 + 16] for tile in range(tiles)]
            accs = [jnp.zeros((16, tokens), bf16)] * tiles
            for slot in range(slots):
                pick, score = pick_wide_ref[slot], score_wide_ref[slot]
                accs = [jnp.where(code == pick, score, acc) for code, acc in zip(codes, accs)]
            for tile in range(tiles):
                start = pl.multiple_of(at * block + tile * 16, 16)
                sub_ref[half, pl.ds(start, 16), :] = accs[tile]
            return carry

        lax.fori_loop(0, subs // block, one, 0)
    dests = out_ref.shape[0]
    own = subs // dests
    layer = layer_ref[...]
    for half in range(halves):
        dquery = lax.dot_general(
            sub_ref[half], keys_ref[half], (((0,), (0,)), ((), ())), preferred_element_type=f32
        ).astype(bf16)
        proj = lax.dot_general(
            dquery, layer, (((0,), (0,)), ((), ())), preferred_element_type=f32
        ).astype(bf16)
        per = width // own
        for at in range(per):
            out_ref[half * per + at, :own, :] = proj[at * own : at * own + own]
    fetch.wait()
    key = jnp.dot(sub_ref[quarter >> 1], mine_ref[...], preferred_element_type=f32).astype(bf16)
    for at in range(dests):
        out_ref[at, own:, :] = key[at * own : at * own + own]


def sum_kernel(first, parts_ref, out_ref):
    rows = slice(first, first + out_ref.shape[0])
    total = parts_ref[0, rows, :].astype(f32)
    for at in range(1, parts_ref.shape[0]):
        total = total + parts_ref[at, rows, :].astype(f32)
    out_ref[...] = total.astype(out_ref.dtype)


def join_kernel(own_ref, one_ref, two_ref, three_ref, out_ref):
    quarter = lax.axis_index("mem") & 3
    cut = own_ref.shape[1]
    for at, ref in enumerate((own_ref, one_ref, two_ref, three_ref)):
        there = quarter ^ at
        out_ref[there >> 1, :, pl.ds(pl.multiple_of((there & 1) * cut, cut), cut)] = ref[...].astype(f32)


def swap(x, mask, count):
    return lax.ppermute(x, "mem", [(at, at ^ mask) for at in range(count)])


def body(grad_out, values, slot_rows, weights, sub_picks, queries, sub_keys, layer_input):
    groups = lax.axis_size("dp")
    mem_count = lax.axis_size("mem")
    tokens, width = grad_out.shape
    slots = slot_rows.shape[1]
    val_rows = values.shape[0]
    halves, subs, key_width = sub_keys.shape
    weights_t = weights.T
    rows_t = slot_rows.T
    picks_t = jnp.swapaxes(sub_picks, 1, 2)

    def along_x(x, shift):
        return lax.ppermute(
            x, "dp", [(at, at // SIDE * SIDE + (at + shift) % SIDE) for at in range(groups)]
        )

    columns = [[row * SIDE + column for row in range(SIDE)] for column in range(SIDE)]

    near_values = [values] + [along_x(values, shift) for shift in (1, 2, 3)]
    sent = run(
        pack_kernel,
        shape((SIDE, tokens + slots, width), bf16),
        (grad_out, rows_t, weights_t),
        scratch=(
            pltpu.VMEM((tokens + slots, width), bf16),
            pltpu.VMEM((slots, tokens), jnp.int32),
            pltpu.VMEM((slots, tokens), f32),
            pltpu.SemaphoreType.DMA((3,)),
            pltpu.SemaphoreType.DMA((SIDE,)),
        ),
        far=(0, 1, 2),
        out_spec=FAR,
        room=60,
    )
    recv = lax.all_to_all(sent, "dp", 0, 0, tiled=True, axis_index_groups=columns)
    slot_parts = run(
        slot_kernel, shape((SIDE, slots, tokens), f32), (recv, *near_values), flops=10**9, data=2**20
    )
    slot_parts = lax.all_to_all(slot_parts, "dp", 0, 0, tiled=True, axis_index_groups=columns)
    slot_grad = jnp.sum(slot_parts, axis=0)

    def value_part(shifts):
        kinds = [shape((val_rows, width), bf16 if shift else f32) for shift in shifts]
        return run(
            functools.partial(value_kernel, shifts),
            kinds,
            (recv,),
            scratch=(
                pltpu.VMEM((SIDE, slots, tokens), f32),
                pltpu.VMEM((SIDE, slots, tokens), f32),
                pltpu.VMEM((val_rows, SIDE * tokens), bf16),
                pltpu.VMEM((SIDE * tokens, width), bf16),
            ),
            flops=2 * 10**9,
            data=2**20,
        )

    slot_grad, recv = lax.optimization_barrier((slot_grad, recv))
    one, two, three = (swap(slot_grad, mask, mem_count) for mask in (1, 2, 3))
    away = value_part((2, 1))
    slot_grad = (slot_grad + one) + (two + three)
    slot_grad, recv, *away = lax.optimization_barrier((slot_grad, recv, *away))
    sums = [along_x(away[0], 2), along_x(away[1], 1)]
    last, mine = value_part((3, 0))
    slot_grad = slot_grad + swap(slot_grad, 4, mem_count)
    slot_grad, last, mine = lax.optimization_barrier((slot_grad, last, mine))
    sums.append(along_x(last, 3))
    slot_grad = slot_grad + swap(slot_grad, 12, mem_count)
    slot_grad, mine, *sums = lax.optimization_barrier((slot_grad, mine, *sums))

    own = subs // groups
    parts = run(
        part_kernel,
        shape((groups, 2 * own, width), bf16),
        (slot_grad, weights_t, picks_t, queries, sub_keys, layer_input),
        scratch=(
            pltpu.VMEM((2, slots, tokens), f32),
            pltpu.VMEM((slots, tokens), f32),
            pltpu.VMEM((slots, 16, tokens), bf16),
            pltpu.VMEM((slots, 16, tokens), bf16),
            pltpu.VMEM((halves, subs, tokens), bf16),
            pltpu.VMEM((tokens, queries.shape[1] // 4), bf16),
            pltpu.SemaphoreType.DMA(()),
        ),
        far=(3,),
    )
    parts = lax.all_to_all(parts, "dp", 0, 0, tiled=True)
    key = run(functools.partial(sum_kernel, own), shape((own, width), bf16), (parts,))
    key, mine, *sums = lax.optimization_barrier((key, mine, *sums))
    others = [swap(key, mask, mem_count) for mask in (1, 2, 3)]
    proj_grad = run(
        functools.partial(sum_kernel, 0),
        shape((own, width), f32),
        (parts,),
        flops=10**9,
        data=2**19,
    )
    value_grad = run(
        add_kernel, shape((val_rows, width), f32), (mine, *sums), flops=10**9, data=2**19
    )
    key_grad = run(join_kernel, shape((halves, own, key_width), f32), (key, *others))
    return (value_grad, key_grad, proj_grad)


def solution(mesh):
    return jax.shard_map(
        body,
        mesh=mesh,
        in_specs=(
            P("dp", "mem"),
            P("dp", "mem"),
            P("dp", None),
            P("dp", None),
            P(None, "dp", None),
            P("dp", None),
            P(),
            P("dp", "mem"),
        ),
        out_specs=(P("dp", "mem"), P(None, "dp", None), P("dp", "mem")),
        check_vma=False,
    )
```

```python
import functools

import jax
import jax.numpy as jnp
from jax import lax
from jax.experimental import pallas as pl
from jax.experimental.pallas import tpu as pltpu
from jax.sharding import PartitionSpec as P


f32 = jnp.float32
bf16 = jnp.bfloat16
SIDE = 4
VM = pl.BlockSpec(memory_space=pltpu.VMEM)
FAR = pl.BlockSpec(memory_space=pltpu.HBM)


def run(kernel, outs, args, scratch=(), flops=0, data=0, far=(), out_spec=VM, room=16):
    return pl.pallas_call(
        kernel,
        out_shape=outs,
        in_specs=[FAR if at in far else VM for at in range(len(args))],
        out_specs=jax.tree.map(lambda _: out_spec, outs),
        scratch_shapes=list(scratch),
        cost_estimate=pl.CostEstimate(flops=flops, bytes_accessed=data, transcendentals=0),
        compiler_params=pltpu.CompilerParams(vmem_limit_bytes=room * 2**20),
    )(*args)


def shape(dims, dtype):
    return jax.ShapeDtypeStruct(dims, dtype)


def row_codes(ids):
    power = ids >> 7
    scale = (1 << (power & 15)).astype(f32) * jnp.where(power >= 16, 65536.0, 1.0)
    return ((ids & 127) + 128).astype(f32) * scale


def pack_kernel(grad_ref, rows_ref, weights_ref, out_ref, one_ref, ids_ref, wide_ref, in_sem, out_sem):
    tokens = grad_ref.shape[0]
    copies = (
        pltpu.make_async_copy(rows_ref, ids_ref, in_sem.at[0]),
        pltpu.make_async_copy(weights_ref, wide_ref, in_sem.at[1]),
        pltpu.make_async_copy(grad_ref, one_ref.at[pl.ds(0, tokens), :], in_sem.at[2]),
    )
    for copy in copies:
        copy.start()
    copies[0].wait()
    copies[1].wait()
    both = jnp.concatenate([row_codes(ids_ref[...]), wide_ref[...]], axis=1)
    one_ref[tokens:, :] = both.astype(bf16)
    copies[2].wait()
    sends = [
        pltpu.make_async_copy(one_ref, out_ref.at[at], out_sem.at[at])
        for at in range(out_ref.shape[0])
    ]
    for send in sends:
        send.start()
    for send in sends:
        send.wait()


def power_of(base, exponent, bits):
    scale = jnp.float32(1.0)
    for bit in range(bits):
        scale = scale * jnp.where((exponent >> bit) & 1 == 1, base ** (2**bit), 1.0)
    return scale


def group_rows(codes):
    row = lax.axis_index("dp") // SIDE
    moved = codes.astype(f32) * power_of(2.0**-8, row, 2)
    inside = (moved >= 128.0) & (moved < 32768.0)
    local = jnp.full(codes.shape, -128, jnp.int32)
    for step in (4, 2, 1):
        above = moved >= 128.0 * 2.0**step
        moved = jnp.where(above, moved * 2.0**-step, moved)
        local = jnp.where(above, local + 128 * step, local)
    return jnp.where(inside, local + moved.astype(jnp.int32), -1)


def slot_kernel(recv_ref, own_ref, *refs):
    values_refs, (out_ref, own_here_ref, sem) = refs[:-3], refs[-3:]
    blocks, slots, tokens = out_ref.shape
    val_rows = own_ref.shape[0]
    column = lax.axis_index("dp") % SIDE
    fetch = pltpu.make_async_copy(own_ref, own_here_ref, sem)
    fetch.start()
    rows = [group_rows(recv_ref[at, tokens:, :tokens]) for at in range(blocks)]
    accs = [[jnp.zeros((8, tokens), f32) for _ in range(slots // 8)] for _ in range(blocks)]
    for shift in range(len(values_refs), -1, -1):
        if shift == 0:
            fetch.wait()
        values_ref = values_refs[shift - 1] if shift else own_here_ref
        first = ((column + SIDE - shift) % SIDE) * (val_rows // 8)
        for at in range(blocks):
            score = lax.dot_general(
                values_ref[...],
                recv_ref[at, :tokens, :],
                (((1,), (1,)), ((), ())),
                preferred_element_type=f32,
            )
            for part in range(slots // 8):
                row = rows[at][part * 8 : part * 8 + 8]
                low, high = row & 7, (row >> 3) - first
                for tile in range(val_rows // 8):
                    got = jnp.take_along_axis(score[tile * 8 : tile * 8 + 8], low, axis=0)
                    accs[at][part] = jnp.where(high == tile, got, accs[at][part])
    for at in range(blocks):
        for part in range(slots // 8):
            out_ref[at, part * 8 : part * 8 + 8, :] = accs[at][part]


def wide_row(ref, at):
    return jnp.broadcast_to(ref[at, :][None, :], (16, ref.shape[1])).astype(bf16)


def value_kernel(shifts, recv_ref, *refs):
    out_refs, (rows_ref, wide_ref, bag_ref, grads_ref) = refs[:-4], refs[-4:]
    blocks = recv_ref.shape[0]
    val_rows = out_refs[0].shape[0]
    slots, tokens = rows_ref.shape[1:]
    tiles = val_rows // 16
    owner = lax.axis_index("dp")
    row, column = owner // SIDE, owner % SIDE
    base = row_codes(lax.broadcasted_iota(jnp.int32, (val_rows, tokens), 0))
    for at in range(blocks):
        rows_ref[at] = recv_ref[at, tokens:, :tokens].astype(f32)
        wide_ref[at] = recv_ref[at, tokens:, tokens:].astype(f32)
        grads_ref[at * tokens : at * tokens + tokens, :] = recv_ref[at, :tokens, :]
    for shift, out_ref in zip(shifts, out_refs):
        holder = row * SIDE + (column + shift) % SIDE
        codes = (base * power_of(4.0, holder, 4)).astype(bf16)
        codes = [codes[tile * 16 : tile * 16 + 16] for tile in range(tiles)]

        def one(at, carry, codes=codes):
            span = pl.ds(pl.multiple_of(at * tokens, tokens), tokens)
            bags = [jnp.zeros((16, tokens), bf16)] * tiles
            for slot in range(slots):
                code_now = wide_row(rows_ref.at[at], slot)
                weight = wide_row(wide_ref.at[at], slot)
                bags = [jnp.where(code == code_now, weight, bag) for code, bag in zip(codes, bags)]
            for tile in range(tiles):
                bag_ref[tile * 16 : tile * 16 + 16, span] = bags[tile]
            return carry

        lax.fori_loop(0, blocks, one, 0)
        total = jnp.dot(bag_ref[...], grads_ref[...], preferred_element_type=f32)
        out_ref[...] = total.astype(out_ref.dtype)


def add_kernel(*refs):
    total = refs[0][...].astype(f32)
    for ref in refs[1:-1]:
        total = total + ref[...].astype(f32)
    refs[-1][...] = total


def part_kernel(
    slot_ref,
    weights_ref,
    picks_ref,
    queries_ref,
    keys_ref,
    layer_ref,
    out_ref,
    score_ref,
    pick_code_ref,
    pick_wide_ref,
    score_wide_ref,
    sub_ref,
    mine_ref,
    sem,
):
    slots, tokens = slot_ref.shape
    halves, subs, width = keys_ref.shape
    quarter = lax.axis_index("mem") & 3
    cut = mine_ref.shape[1]
    fetch = pltpu.make_async_copy(
        queries_ref.at[:, pl.ds(pl.multiple_of(quarter * cut, cut), cut)], mine_ref, sem
    )
    fetch.start()
    weights = weights_ref[...]
    slot_grad = slot_ref[...]
    centered = slot_grad - jnp.sum(weights * slot_grad, axis=0, keepdims=True)
    score_ref[0] = weights * centered
    block = 128
    tiles = block // 16
    base = lax.broadcasted_iota(jnp.int32, (block, tokens), 0).astype(f32) + 128.0
    for half in range(halves):
        picks = picks_ref[half]
        merged = jnp.zeros((slots, tokens), f32)
        for slot in range(slots):
            same = picks == picks_ref[half, slot : slot + 1, :]
            merged = merged + jnp.where(same, score_ref[0, slot : slot + 1, :], 0.0)
        score_ref[1] = merged
        pick_code_ref[...] = row_codes(picks)
        for slot in range(slots):
            pick_wide_ref[slot] = wide_row(pick_code_ref, slot)
            score_wide_ref[slot] = wide_row(score_ref.at[1], slot)

        def one(at, carry, half=half):
            codes = (base * (1 << at).astype(f32)).astype(bf16)
            codes = [codes[tile * 16 : tile * 16 + 16] for tile in range(tiles)]
            accs = [jnp.zeros((16, tokens), bf16)] * tiles
            for slot in range(slots):
                pick, score = pick_wide_ref[slot], score_wide_ref[slot]
                accs = [jnp.where(code == pick, score, acc) for code, acc in zip(codes, accs)]
            for tile in range(tiles):
                start = pl.multiple_of(at * block + tile * 16, 16)
                sub_ref[half, pl.ds(start, 16), :] = accs[tile]
            return carry

        lax.fori_loop(0, subs // block, one, 0)
    dests = out_ref.shape[0]
    own = subs // dests
    layer = layer_ref[...]
    for half in range(halves):
        dquery = lax.dot_general(
            sub_ref[half], keys_ref[half], (((0,), (0,)), ((), ())), preferred_element_type=f32
        ).astype(bf16)
        proj = lax.dot_general(
            dquery, layer, (((0,), (0,)), ((), ())), preferred_element_type=f32
        ).astype(bf16)
        per = width // own
        for at in range(per):
            out_ref[half * per + at, :own, :] = proj[at * own : at * own + own]
    fetch.wait()
    key = jnp.dot(sub_ref[quarter >> 1], mine_ref[...], preferred_element_type=f32).astype(bf16)
    for at in range(dests):
        out_ref[at, own:, :] = key[at * own : at * own + own]


def sum_kernel(first, parts_ref, out_ref):
    rows = slice(first, first + out_ref.shape[0])
    total = parts_ref[0, rows, :].astype(f32)
    for at in range(1, parts_ref.shape[0]):
        total = total + parts_ref[at, rows, :].astype(f32)
    out_ref[...] = total.astype(out_ref.dtype)


def join_kernel(own_ref, one_ref, two_ref, three_ref, out_ref):
    quarter = lax.axis_index("mem") & 3
    cut = own_ref.shape[1]
    for at, ref in enumerate((own_ref, one_ref, two_ref, three_ref)):
        there = quarter ^ at
        out_ref[there >> 1, :, pl.ds(pl.multiple_of((there & 1) * cut, cut), cut)] = ref[...].astype(f32)


def swap(x, mask, count):
    return lax.ppermute(x, "mem", [(at, at ^ mask) for at in range(count)])


def step_body(grad_out, values, slot_rows, weights, sub_picks, queries, sub_keys, layer_input):
    groups = lax.axis_size("dp")
    mem_count = lax.axis_size("mem")
    tokens, width = grad_out.shape
    slots = slot_rows.shape[1]
    val_rows = values.shape[0]
    halves, subs, key_width = sub_keys.shape
    weights_t = weights.T
    rows_t = slot_rows.T
    picks_t = jnp.swapaxes(sub_picks, 1, 2)

    def along_x(x, shift):
        return lax.ppermute(
            x, "dp", [(at, at // SIDE * SIDE + (at + shift) % SIDE) for at in range(groups)]
        )

    columns = [[row * SIDE + column for row in range(SIDE)] for column in range(SIDE)]

    near_values = [along_x(values, shift) for shift in (1, 2, 3)]
    sent = run(
        pack_kernel,
        shape((SIDE, tokens + slots, width), bf16),
        (grad_out, rows_t, weights_t),
        scratch=(
            pltpu.VMEM((tokens + slots, width), bf16),
            pltpu.VMEM((slots, tokens), jnp.int32),
            pltpu.VMEM((slots, tokens), f32),
            pltpu.SemaphoreType.DMA((3,)),
            pltpu.SemaphoreType.DMA((SIDE,)),
        ),
        far=(0, 1, 2),
        out_spec=FAR,
        room=60,
    )
    recv = lax.all_to_all(sent, "dp", 0, 0, tiled=True, axis_index_groups=columns)
    shifts = (2, 1, 3, 0)
    away = run(
        functools.partial(value_kernel, shifts),
        [shape((val_rows, width), bf16 if shift else f32) for shift in shifts],
        (recv,),
        scratch=(
            pltpu.VMEM((SIDE, slots, tokens), f32),
            pltpu.VMEM((SIDE, slots, tokens), f32),
            pltpu.VMEM((val_rows, SIDE * tokens), bf16),
            pltpu.VMEM((SIDE * tokens, width), bf16),
        ),
        flops=4 * 10**9,
        data=2**21,
    )
    near = lax.optimization_barrier((*near_values, *away))
    near_values, (two_away, one_away, three_away, mine) = near[:3], near[3:]
    slot_parts = run(
        slot_kernel,
        shape((SIDE, slots, tokens), f32),
        (recv, values, *near_values),
        scratch=(pltpu.VMEM((val_rows, width), bf16), pltpu.SemaphoreType.DMA(())),
        flops=10**9,
        data=2**20,
        far=(1,),
    )
    slot_parts = lax.all_to_all(slot_parts, "dp", 0, 0, tiled=True, axis_index_groups=columns)
    slot_grad = jnp.sum(slot_parts, axis=0)

    one, two, three = (swap(slot_grad, mask, mem_count) for mask in (1, 2, 3))
    slot_grad = (slot_grad + one) + (two + three)
    slot_grad, two_away, one_away, three_away = lax.optimization_barrier(
        (slot_grad, two_away, one_away, three_away)
    )
    sums = [along_x(two_away, 2), along_x(one_away, 1)]
    sums.append(along_x(three_away, 3))
    step = swap(slot_grad, 4, mem_count)
    slot_grad = slot_grad + step
    step = swap(slot_grad, 12, mem_count)
    slot_grad = slot_grad + step

    own = subs // groups
    parts = run(
        part_kernel,
        shape((groups, 2 * own, width), bf16),
        (slot_grad, weights_t, picks_t, queries, sub_keys, layer_input),
        scratch=(
            pltpu.VMEM((2, slots, tokens), f32),
            pltpu.VMEM((slots, tokens), f32),
            pltpu.VMEM((slots, 16, tokens), bf16),
            pltpu.VMEM((slots, 16, tokens), bf16),
            pltpu.VMEM((halves, subs, tokens), bf16),
            pltpu.VMEM((tokens, queries.shape[1] // 4), bf16),
            pltpu.SemaphoreType.DMA(()),
        ),
        far=(3,),
    )
    parts, mine, *sums = lax.optimization_barrier((parts, mine, *sums))
    parts = lax.all_to_all(parts, "dp", 0, 0, tiled=True)
    key = run(functools.partial(sum_kernel, own), shape((own, width), bf16), (parts,))
    key, mine, *sums = lax.optimization_barrier((key, mine, *sums))
    others = [swap(key, mask, mem_count) for mask in (1, 2, 3)]
    proj_grad = run(
        functools.partial(sum_kernel, 0),
        shape((own, width), f32),
        (parts,),
        flops=10**9,
        data=2**19,
    )
    value_grad = run(
        add_kernel, shape((val_rows, width), f32), (mine, *sums), flops=10**9, data=2**19
    )
    key_grad = run(join_kernel, shape((halves, own, key_width), f32), (key, *others))
    return (value_grad, key_grad, proj_grad)


def solution(mesh):
    return jax.shard_map(
        step_body,
        mesh=mesh,
        in_specs=(
            P("dp", "mem"),
            P("dp", "mem"),
            P("dp", None),
            P("dp", None),
            P(None, "dp", None),
            P("dp", None),
            P(),
            P("dp", "mem"),
        ),
        out_specs=(P("dp", "mem"), P(None, "dp", None), P("dp", "mem")),
        check_vma=False,
    )
```

```python
import functools

import jax
import jax.numpy as jnp
from jax import lax
from jax.experimental import pallas as pl
from jax.experimental.pallas import tpu as pltpu
from jax.sharding import PartitionSpec as P


f32 = jnp.float32
bf16 = jnp.bfloat16
SIDE = 4
VM = pl.BlockSpec(memory_space=pltpu.VMEM)
FAR = pl.BlockSpec(memory_space=pltpu.HBM)


def run(kernel, outs, args, scratch=(), flops=0, data=0, far=()):
    return pl.pallas_call(
        kernel,
        out_shape=outs,
        in_specs=[FAR if at in far else VM for at in range(len(args))],
        out_specs=jax.tree.map(lambda _: VM, outs),
        scratch_shapes=list(scratch),
        cost_estimate=pl.CostEstimate(flops=flops, bytes_accessed=data, transcendentals=0),
        compiler_params=pltpu.CompilerParams(vmem_limit_bytes=16 * 2**20),
    )(*args)


def shape(dims, dtype):
    return jax.ShapeDtypeStruct(dims, dtype)


def row_codes(ids):
    power = ids >> 7
    scale = (1 << (power & 15)).astype(f32) * jnp.where(power >= 16, 65536.0, 1.0)
    return ((ids & 127) + 128).astype(f32) * scale


def pack_kernel(grad_ref, rows_ref, weights_ref, out_ref, ids_ref, wide_ref, sems):
    tokens = grad_ref.shape[0]
    copies = [
        pltpu.make_async_copy(rows_ref, ids_ref, sems.at[0]),
        pltpu.make_async_copy(weights_ref, wide_ref, sems.at[1]),
    ]
    for at in range(out_ref.shape[0]):
        here = out_ref.at[at, pl.ds(0, tokens), :]
        copies.append(pltpu.make_async_copy(grad_ref, here, sems.at[2 + at]))
    for copy in copies:
        copy.start()
    copies[0].wait()
    copies[1].wait()
    both = jnp.concatenate([row_codes(ids_ref[...]), wide_ref[...]], axis=1).astype(bf16)
    for at in range(out_ref.shape[0]):
        out_ref[at, tokens:, :] = both
    for copy in copies[2:]:
        copy.wait()


def power_of(base, exponent, bits):
    scale = jnp.float32(1.0)
    for bit in range(bits):
        scale = scale * jnp.where((exponent >> bit) & 1 == 1, base ** (2**bit), 1.0)
    return scale


def group_rows(codes):
    row = lax.axis_index("dp") // SIDE
    moved = codes.astype(f32) * power_of(2.0**-8, row, 2)
    inside = (moved >= 128.0) & (moved < 32768.0)
    local = jnp.full(codes.shape, -128, jnp.int32)
    for step in (4, 2, 1):
        above = moved >= 128.0 * 2.0**step
        moved = jnp.where(above, moved * 2.0**-step, moved)
        local = jnp.where(above, local + 128 * step, local)
    return jnp.where(inside, local + moved.astype(jnp.int32), -1)


def slot_kernel(recv_ref, own_ref, *refs):
    values_refs, (out_ref, own_here_ref, sem) = refs[:-3], refs[-3:]
    blocks, slots, tokens = out_ref.shape
    val_rows = own_ref.shape[0]
    column = lax.axis_index("dp") % SIDE
    fetch = pltpu.make_async_copy(own_ref, own_here_ref, sem)
    fetch.start()
    rows = [group_rows(recv_ref[at, tokens:, :tokens]) for at in range(blocks)]
    accs = [[jnp.zeros((8, tokens), f32) for _ in range(slots // 8)] for _ in range(blocks)]
    for shift in range(len(values_refs), -1, -1):
        if shift == 0:
            fetch.wait()
        values_ref = values_refs[shift - 1] if shift else own_here_ref
        first = ((column + SIDE - shift) % SIDE) * (val_rows // 8)
        for at in range(blocks):
            score = lax.dot_general(
                values_ref[...],
                recv_ref[at, :tokens, :],
                (((1,), (1,)), ((), ())),
                preferred_element_type=f32,
            )
            for part in range(slots // 8):
                row = rows[at][part * 8 : part * 8 + 8]
                low, high = row & 7, (row >> 3) - first
                for tile in range(val_rows // 8):
                    got = jnp.take_along_axis(score[tile * 8 : tile * 8 + 8], low, axis=0)
                    accs[at][part] = jnp.where(high == tile, got, accs[at][part])
    for at in range(blocks):
        for part in range(slots // 8):
            out_ref[at, part * 8 : part * 8 + 8, :] = accs[at][part]


def wide_row(ref, at):
    return jnp.broadcast_to(ref[at, :][None, :], (16, ref.shape[1])).astype(bf16)


def value_kernel(shifts, recv_ref, *refs):
    out_refs, (rows_ref, wide_ref, bag_ref, grads_ref) = refs[:-4], refs[-4:]
    blocks = recv_ref.shape[0]
    val_rows = out_refs[0].shape[0]
    slots, tokens = rows_ref.shape[1:]
    tiles = val_rows // 16
    owner = lax.axis_index("dp")
    row, column = owner // SIDE, owner % SIDE
    base = row_codes(lax.broadcasted_iota(jnp.int32, (val_rows, tokens), 0))
    for at in range(blocks):
        rows_ref[at] = recv_ref[at, tokens:, :tokens].astype(f32)
        wide_ref[at] = recv_ref[at, tokens:, tokens:].astype(f32)
        grads_ref[at * tokens : at * tokens + tokens, :] = recv_ref[at, :tokens, :]
    for shift, out_ref in zip(shifts, out_refs):
        holder = row * SIDE + (column + shift) % SIDE
        codes = (base * power_of(4.0, holder, 4)).astype(bf16)
        codes = [codes[tile * 16 : tile * 16 + 16] for tile in range(tiles)]

        def one(at, carry, codes=codes):
            span = pl.ds(pl.multiple_of(at * tokens, tokens), tokens)
            bags = [jnp.zeros((16, tokens), bf16)] * tiles
            for slot in range(slots):
                code_now = wide_row(rows_ref.at[at], slot)
                weight = wide_row(wide_ref.at[at], slot)
                bags = [jnp.where(code == code_now, weight, bag) for code, bag in zip(codes, bags)]
            for tile in range(tiles):
                bag_ref[tile * 16 : tile * 16 + 16, span] = bags[tile]
            return carry

        lax.fori_loop(0, blocks, one, 0)
        total = jnp.dot(bag_ref[...], grads_ref[...], preferred_element_type=f32)
        out_ref[...] = total.astype(out_ref.dtype)


def add_kernel(*refs):
    total = refs[0][...].astype(f32)
    for ref in refs[1:-1]:
        total = total + ref[...].astype(f32)
    refs[-1][...] = total


def part_kernel(
    slot_ref,
    weights_ref,
    picks_ref,
    queries_ref,
    keys_ref,
    layer_ref,
    out_ref,
    score_ref,
    pick_code_ref,
    pick_wide_ref,
    score_wide_ref,
    sub_ref,
    mine_ref,
    sem,
):
    slots, tokens = slot_ref.shape
    halves, subs, width = keys_ref.shape
    quarter = lax.axis_index("mem") & 3
    cut = mine_ref.shape[1]
    fetch = pltpu.make_async_copy(
        queries_ref.at[:, pl.ds(pl.multiple_of(quarter * cut, cut), cut)], mine_ref, sem
    )
    fetch.start()
    weights = weights_ref[...]
    slot_grad = slot_ref[...]
    centered = slot_grad - jnp.sum(weights * slot_grad, axis=0, keepdims=True)
    score_ref[0] = weights * centered
    block = 128
    tiles = block // 16
    base = lax.broadcasted_iota(jnp.int32, (block, tokens), 0).astype(f32) + 128.0
    for half in range(halves):
        picks = picks_ref[half]
        merged = jnp.zeros((slots, tokens), f32)
        for slot in range(slots):
            same = picks == picks_ref[half, slot : slot + 1, :]
            merged = merged + jnp.where(same, score_ref[0, slot : slot + 1, :], 0.0)
        score_ref[1] = merged
        pick_code_ref[...] = row_codes(picks)
        for slot in range(slots):
            pick_wide_ref[slot] = wide_row(pick_code_ref, slot)
            score_wide_ref[slot] = wide_row(score_ref.at[1], slot)

        def one(at, carry, half=half):
            codes = (base * (1 << at).astype(f32)).astype(bf16)
            codes = [codes[tile * 16 : tile * 16 + 16] for tile in range(tiles)]
            accs = [jnp.zeros((16, tokens), bf16)] * tiles
            for slot in range(slots):
                pick, score = pick_wide_ref[slot], score_wide_ref[slot]
                accs = [jnp.where(code == pick, score, acc) for code, acc in zip(codes, accs)]
            for tile in range(tiles):
                start = pl.multiple_of(at * block + tile * 16, 16)
                sub_ref[half, pl.ds(start, 16), :] = accs[tile]
            return carry

        lax.fori_loop(0, subs // block, one, 0)
    dests = out_ref.shape[0]
    own = subs // dests
    layer = layer_ref[...]
    for half in range(halves):
        dquery = lax.dot_general(
            sub_ref[half], keys_ref[half], (((0,), (0,)), ((), ())), preferred_element_type=f32
        ).astype(bf16)
        proj = lax.dot_general(
            dquery, layer, (((0,), (0,)), ((), ())), preferred_element_type=f32
        ).astype(bf16)
        per = width // own
        for at in range(per):
            out_ref[half * per + at, :own, :] = proj[at * own : at * own + own]
    fetch.wait()
    key = jnp.dot(sub_ref[quarter >> 1], mine_ref[...], preferred_element_type=f32).astype(bf16)
    for at in range(dests):
        out_ref[at, own:, :] = key[at * own : at * own + own]


def sum_kernel(first, parts_ref, out_ref):
    rows = slice(first, first + out_ref.shape[0])
    total = parts_ref[0, rows, :].astype(f32)
    for at in range(1, parts_ref.shape[0]):
        total = total + parts_ref[at, rows, :].astype(f32)
    out_ref[...] = total.astype(out_ref.dtype)


def join_kernel(own_ref, one_ref, two_ref, three_ref, out_ref):
    quarter = lax.axis_index("mem") & 3
    cut = own_ref.shape[1]
    for at, ref in enumerate((own_ref, one_ref, two_ref, three_ref)):
        there = quarter ^ at
        out_ref[there >> 1, :, pl.ds(pl.multiple_of((there & 1) * cut, cut), cut)] = ref[...].astype(f32)


def stay(x):
    return pltpu.with_memory_space_constraint(x, pltpu.HBM)


def swap(x, mask, count):
    return lax.ppermute(x, "mem", [(at, at ^ mask) for at in range(count)])


def step_body(grad_out, values, slot_rows, weights, sub_picks, queries, sub_keys, layer_input):
    groups = lax.axis_size("dp")
    mem_count = lax.axis_size("mem")
    tokens, width = grad_out.shape
    slots = slot_rows.shape[1]
    val_rows = values.shape[0]
    halves, subs, key_width = sub_keys.shape
    weights_t = weights.T
    rows_t = slot_rows.T
    picks_t = jnp.swapaxes(sub_picks, 1, 2)

    def along_x(x, shift):
        return lax.ppermute(
            x, "dp", [(at, at // SIDE * SIDE + (at + shift) % SIDE) for at in range(groups)]
        )

    columns = [[row * SIDE + column for row in range(SIDE)] for column in range(SIDE)]

    far_values = along_x(values, 2)
    near_values = [along_x(values, 1), far_values, along_x(values, 3)]
    sent = run(
        pack_kernel,
        shape((SIDE, tokens + slots, width), bf16),
        [stay(x) for x in (grad_out, rows_t, weights_t)],
        scratch=(
            pltpu.VMEM((slots, tokens), jnp.int32),
            pltpu.VMEM((slots, tokens), f32),
            pltpu.SemaphoreType.DMA((2 + SIDE,)),
        ),
        far=(0, 1, 2),
    )
    recv = lax.all_to_all(sent, "dp", 0, 0, tiled=True, axis_index_groups=columns)

    def value_part(shifts, recv):
        return run(
            functools.partial(value_kernel, shifts),
            [shape((val_rows, width), bf16 if shift else f32) for shift in shifts],
            (recv,),
            scratch=(
                pltpu.VMEM((SIDE, slots, tokens), f32),
                pltpu.VMEM((SIDE, slots, tokens), f32),
                pltpu.VMEM((val_rows, SIDE * tokens), bf16),
                pltpu.VMEM((SIDE * tokens, width), bf16),
            ),
            flops=2 * 10**9,
            data=2**20,
        )

    slot_parts = run(
        slot_kernel,
        shape((SIDE, slots, tokens), f32),
        (recv, stay(values), *near_values),
        scratch=(pltpu.VMEM((val_rows, width), bf16), pltpu.SemaphoreType.DMA(())),
        flops=10**9,
        data=2**20,
        far=(1,),
    )
    slot_parts = lax.all_to_all(slot_parts, "dp", 0, 0, tiled=True, axis_index_groups=columns)
    slot_grad = jnp.sum(slot_parts, axis=0)

    slot_grad, recv = lax.optimization_barrier((slot_grad, recv))
    one, two, three = (swap(slot_grad, mask, mem_count) for mask in (1, 2, 3))
    two_away, one_away = value_part((2, 1), recv)
    slot_grad = (slot_grad + one) + (two + three)
    slot_grad, recv, two_away, one_away = lax.optimization_barrier(
        (slot_grad, recv, two_away, one_away)
    )
    step = swap(slot_grad, 4, mem_count)
    sums = [along_x(two_away, 2), along_x(one_away, 1)]
    slot_grad = slot_grad + step
    slot_grad, recv = lax.optimization_barrier((slot_grad, recv))
    step = swap(slot_grad, 12, mem_count)
    three_away, mine = value_part((3, 0), recv)
    slot_grad = slot_grad + step
    sums.append(along_x(three_away, 3))

    own = subs // groups
    parts = run(
        part_kernel,
        shape((groups, 2 * own, width), bf16),
        (slot_grad, weights_t, picks_t, queries, sub_keys, layer_input),
        scratch=(
            pltpu.VMEM((2, slots, tokens), f32),
            pltpu.VMEM((slots, tokens), f32),
            pltpu.VMEM((slots, 16, tokens), bf16),
            pltpu.VMEM((slots, 16, tokens), bf16),
            pltpu.VMEM((halves, subs, tokens), bf16),
            pltpu.VMEM((tokens, queries.shape[1] // 4), bf16),
            pltpu.SemaphoreType.DMA(()),
        ),
        far=(3,),
    )
    parts, mine, *sums = lax.optimization_barrier((parts, mine, *sums))
    parts = lax.all_to_all(parts, "dp", 0, 0, tiled=True)
    key = run(functools.partial(sum_kernel, own), shape((own, width), bf16), (parts,))
    key, mine, *sums = lax.optimization_barrier((key, mine, *sums))
    others = [swap(key, mask, mem_count) for mask in (1, 2, 3)]
    proj_grad = run(
        functools.partial(sum_kernel, 0),
        shape((own, width), f32),
        (parts,),
        flops=10**9,
        data=2**19,
    )
    value_grad = run(
        add_kernel, shape((val_rows, width), f32), (mine, *sums), flops=10**9, data=2**19
    )
    key_grad = run(join_kernel, shape((halves, own, key_width), f32), (key, *others))
    return (value_grad, key_grad, proj_grad)


def solution(mesh):
    return jax.shard_map(
        step_body,
        mesh=mesh,
        in_specs=(
            P("dp", "mem"),
            P("dp", "mem"),
            P("dp", None),
            P("dp", None),
            P(None, "dp", None),
            P("dp", None),
            P(),
            P("dp", "mem"),
        ),
        out_specs=(P("dp", "mem"), P(None, "dp", None), P("dp", "mem")),
        check_vma=False,
    )
```

```python
import functools

import jax
import jax.numpy as jnp
from jax import lax
from jax.experimental import pallas as pl
from jax.experimental.pallas import tpu as pltpu
from jax.sharding import PartitionSpec as P


f32 = jnp.float32
bf16 = jnp.bfloat16
SIDE = 4
VM = pl.BlockSpec(memory_space=pltpu.VMEM)
FAR = pl.BlockSpec(memory_space=pltpu.HBM)


def run(kernel, outs, args, scratch=(), flops=0, data=0, far=()):
    return pl.pallas_call(
        kernel,
        out_shape=outs,
        in_specs=[FAR if at in far else VM for at in range(len(args))],
        out_specs=jax.tree.map(lambda _: VM, outs),
        scratch_shapes=list(scratch),
        cost_estimate=pl.CostEstimate(flops=flops, bytes_accessed=data, transcendentals=0),
        compiler_params=pltpu.CompilerParams(vmem_limit_bytes=16 * 2**20),
    )(*args)


def shape(dims, dtype):
    return jax.ShapeDtypeStruct(dims, dtype)


def row_codes(ids):
    power = ids >> 7
    scale = (1 << (power & 15)).astype(f32) * jnp.where(power >= 16, 65536.0, 1.0)
    return ((ids & 127) + 128).astype(f32) * scale


def pack_kernel(grad_ref, rows_ref, weights_ref, out_ref, ids_ref, wide_ref, sems):
    tokens = grad_ref.shape[0]
    copies = [
        pltpu.make_async_copy(rows_ref, ids_ref, sems.at[0]),
        pltpu.make_async_copy(weights_ref, wide_ref, sems.at[1]),
    ]
    for at in range(out_ref.shape[0]):
        here = out_ref.at[at, pl.ds(0, tokens), :]
        copies.append(pltpu.make_async_copy(grad_ref, here, sems.at[2 + at]))
    for copy in copies:
        copy.start()
    copies[0].wait()
    copies[1].wait()
    both = jnp.concatenate([row_codes(ids_ref[...]), wide_ref[...]], axis=1).astype(bf16)
    for at in range(out_ref.shape[0]):
        out_ref[at, tokens:, :] = both
    for copy in copies[2:]:
        copy.wait()


def power_of(base, exponent, bits):
    scale = jnp.float32(1.0)
    for bit in range(bits):
        scale = scale * jnp.where((exponent >> bit) & 1 == 1, base ** (2**bit), 1.0)
    return scale


def group_rows(codes):
    row = lax.axis_index("dp") // SIDE
    moved = codes.astype(f32) * power_of(2.0**-8, row, 2)
    inside = (moved >= 128.0) & (moved < 32768.0)
    local = jnp.full(codes.shape, -128, jnp.int32)
    for step in (4, 2, 1):
        above = moved >= 128.0 * 2.0**step
        moved = jnp.where(above, moved * 2.0**-step, moved)
        local = jnp.where(above, local + 128 * step, local)
    return jnp.where(inside, local + moved.astype(jnp.int32), -1)


def slot_kernel(recv_ref, own_ref, *refs):
    values_refs, out_refs, (own_here_ref, sem) = refs[: SIDE - 1], refs[SIDE - 1 : -2], refs[-2:]
    slots, tokens = out_refs[0].shape
    val_rows = own_ref.shape[0]
    owner = lax.axis_index("dp")
    row, column = owner // SIDE, owner % SIDE
    fetch = pltpu.make_async_copy(own_ref, own_here_ref, sem)
    fetch.start()
    blocks = [(row + away) % SIDE for away in range(SIDE)]
    local = [group_rows(recv_ref[at, tokens:, :tokens]) for at in blocks]
    accs = [[jnp.zeros((8, tokens), f32) for _ in range(slots // 8)] for _ in blocks]
    for shift in range(SIDE - 1, -1, -1):
        if shift == 0:
            fetch.wait()
        values_ref = values_refs[shift - 1] if shift else own_here_ref
        first = ((column + SIDE - shift) % SIDE) * (val_rows // 8)
        for away, at in enumerate(blocks):
            score = lax.dot_general(
                values_ref[...],
                recv_ref[at, :tokens, :],
                (((1,), (1,)), ((), ())),
                preferred_element_type=f32,
            )
            for part in range(slots // 8):
                rows = local[away][part * 8 : part * 8 + 8]
                low, high = rows & 7, (rows >> 3) - first
                for tile in range(val_rows // 8):
                    got = jnp.take_along_axis(score[tile * 8 : tile * 8 + 8], low, axis=0)
                    accs[away][part] = jnp.where(high == tile, got, accs[away][part])
    for away, out_ref in enumerate(out_refs):
        for part in range(slots // 8):
            out_ref[part * 8 : part * 8 + 8, :] = accs[away][part]


def wide_row(ref, at):
    return jnp.broadcast_to(ref[at, :][None, :], (16, ref.shape[1])).astype(bf16)


def value_kernel(shifts, recv_ref, *refs):
    out_refs, (rows_ref, wide_ref, bag_ref, grads_ref) = refs[:-4], refs[-4:]
    blocks = recv_ref.shape[0]
    val_rows = out_refs[0].shape[0]
    slots, tokens = rows_ref.shape[1:]
    tiles = val_rows // 16
    owner = lax.axis_index("dp")
    row, column = owner // SIDE, owner % SIDE
    base = row_codes(lax.broadcasted_iota(jnp.int32, (val_rows, tokens), 0))
    for at in range(blocks):
        rows_ref[at] = recv_ref[at, tokens:, :tokens].astype(f32)
        wide_ref[at] = recv_ref[at, tokens:, tokens:].astype(f32)
        grads_ref[at * tokens : at * tokens + tokens, :] = recv_ref[at, :tokens, :]
    for shift, out_ref in zip(shifts, out_refs):
        holder = row * SIDE + (column + shift) % SIDE
        codes = (base * power_of(4.0, holder, 4)).astype(bf16)
        codes = [codes[tile * 16 : tile * 16 + 16] for tile in range(tiles)]

        def one(at, carry, codes=codes):
            span = pl.ds(pl.multiple_of(at * tokens, tokens), tokens)
            bags = [jnp.zeros((16, tokens), bf16)] * tiles
            for slot in range(slots):
                code_now = wide_row(rows_ref.at[at], slot)
                weight = wide_row(wide_ref.at[at], slot)
                bags = [jnp.where(code == code_now, weight, bag) for code, bag in zip(codes, bags)]
            for tile in range(tiles):
                bag_ref[tile * 16 : tile * 16 + 16, span] = bags[tile]
            return carry

        lax.fori_loop(0, blocks, one, 0)
        total = jnp.dot(bag_ref[...], grads_ref[...], preferred_element_type=f32)
        out_ref[...] = total.astype(out_ref.dtype)


def add_kernel(*refs):
    total = refs[0][...].astype(f32)
    for ref in refs[1:-1]:
        total = total + ref[...].astype(f32)
    refs[-1][...] = total


def part_kernel(
    slot_ref,
    weights_ref,
    picks_ref,
    queries_ref,
    keys_ref,
    layer_ref,
    out_ref,
    score_ref,
    pick_code_ref,
    pick_wide_ref,
    score_wide_ref,
    sub_ref,
    mine_ref,
    sem,
):
    slots, tokens = slot_ref.shape
    halves, subs, width = keys_ref.shape
    quarter = lax.axis_index("mem") & 3
    cut = mine_ref.shape[1]
    fetch = pltpu.make_async_copy(
        queries_ref.at[:, pl.ds(pl.multiple_of(quarter * cut, cut), cut)], mine_ref, sem
    )
    fetch.start()
    weights = weights_ref[...]
    slot_grad = slot_ref[...]
    centered = slot_grad - jnp.sum(weights * slot_grad, axis=0, keepdims=True)
    score_ref[0] = weights * centered
    block = 128
    tiles = block // 16
    base = lax.broadcasted_iota(jnp.int32, (block, tokens), 0).astype(f32) + 128.0
    for half in range(halves):
        picks = picks_ref[half]
        merged = jnp.zeros((slots, tokens), f32)
        for slot in range(slots):
            same = picks == picks_ref[half, slot : slot + 1, :]
            merged = merged + jnp.where(same, score_ref[0, slot : slot + 1, :], 0.0)
        score_ref[1] = merged
        pick_code_ref[...] = row_codes(picks)
        for slot in range(slots):
            pick_wide_ref[slot] = wide_row(pick_code_ref, slot)
            score_wide_ref[slot] = wide_row(score_ref.at[1], slot)

        def one(at, carry, half=half):
            codes = (base * (1 << at).astype(f32)).astype(bf16)
            codes = [codes[tile * 16 : tile * 16 + 16] for tile in range(tiles)]
            accs = [jnp.zeros((16, tokens), bf16)] * tiles
            for slot in range(slots):
                pick, score = pick_wide_ref[slot], score_wide_ref[slot]
                accs = [jnp.where(code == pick, score, acc) for code, acc in zip(codes, accs)]
            for tile in range(tiles):
                start = pl.multiple_of(at * block + tile * 16, 16)
                sub_ref[half, pl.ds(start, 16), :] = accs[tile]
            return carry

        lax.fori_loop(0, subs // block, one, 0)
    dests = out_ref.shape[0]
    own = subs // dests
    layer = layer_ref[...]
    for half in range(halves):
        dquery = lax.dot_general(
            sub_ref[half], keys_ref[half], (((0,), (0,)), ((), ())), preferred_element_type=f32
        ).astype(bf16)
        proj = lax.dot_general(
            dquery, layer, (((0,), (0,)), ((), ())), preferred_element_type=f32
        ).astype(bf16)
        per = width // own
        for at in range(per):
            out_ref[half * per + at, :own, :] = proj[at * own : at * own + own]
    fetch.wait()
    key = jnp.dot(sub_ref[quarter >> 1], mine_ref[...], preferred_element_type=f32).astype(bf16)
    for at in range(dests):
        out_ref[at, own:, :] = key[at * own : at * own + own]


def sum_kernel(first, parts_ref, out_ref):
    rows = slice(first, first + out_ref.shape[0])
    total = parts_ref[0, rows, :].astype(f32)
    for at in range(1, parts_ref.shape[0]):
        total = total + parts_ref[at, rows, :].astype(f32)
    out_ref[...] = total.astype(out_ref.dtype)


def join_kernel(own_ref, one_ref, two_ref, three_ref, out_ref):
    quarter = lax.axis_index("mem") & 3
    cut = own_ref.shape[1]
    for at, ref in enumerate((own_ref, one_ref, two_ref, three_ref)):
        there = quarter ^ at
        out_ref[there >> 1, :, pl.ds(pl.multiple_of((there & 1) * cut, cut), cut)] = ref[...].astype(f32)


def stay(x):
    return pltpu.with_memory_space_constraint(x, pltpu.HBM)


def swap(x, mask, count):
    return lax.ppermute(x, "mem", [(at, at ^ mask) for at in range(count)])


def step_body(grad_out, values, slot_rows, weights, sub_picks, queries, sub_keys, layer_input):
    groups = lax.axis_size("dp")
    mem_count = lax.axis_size("mem")
    tokens, width = grad_out.shape
    slots = slot_rows.shape[1]
    val_rows = values.shape[0]
    halves, subs, key_width = sub_keys.shape
    weights_t = weights.T
    rows_t = slot_rows.T
    picks_t = jnp.swapaxes(sub_picks, 1, 2)

    def along_x(x, shift):
        return lax.ppermute(
            x, "dp", [(at, at // SIDE * SIDE + (at + shift) % SIDE) for at in range(groups)]
        )

    def along_y(x, shift):
        return lax.ppermute(x, "dp", [(at, (at + shift * SIDE) % groups) for at in range(groups)])

    columns = [[row * SIDE + column for row in range(SIDE)] for column in range(SIDE)]

    far_values = along_x(values, 2)
    near_values = [along_x(values, 1), far_values, along_x(values, 3)]
    sent = run(
        pack_kernel,
        shape((SIDE, tokens + slots, width), bf16),
        [stay(x) for x in (grad_out, rows_t, weights_t)],
        scratch=(
            pltpu.VMEM((slots, tokens), jnp.int32),
            pltpu.VMEM((slots, tokens), f32),
            pltpu.SemaphoreType.DMA((2 + SIDE,)),
        ),
        far=(0, 1, 2),
    )
    recv = lax.all_to_all(sent, "dp", 0, 0, tiled=True, axis_index_groups=columns)

    def value_part(shifts, recv):
        return run(
            functools.partial(value_kernel, shifts),
            [shape((val_rows, width), bf16 if shift else f32) for shift in shifts],
            (recv,),
            scratch=(
                pltpu.VMEM((SIDE, slots, tokens), f32),
                pltpu.VMEM((SIDE, slots, tokens), f32),
                pltpu.VMEM((val_rows, SIDE * tokens), bf16),
                pltpu.VMEM((SIDE * tokens, width), bf16),
            ),
            flops=2 * 10**9,
            data=2**20,
        )

    slot_parts = run(
        slot_kernel,
        [shape((slots, tokens), f32)] * SIDE,
        (recv, stay(values), *near_values),
        scratch=(pltpu.VMEM((val_rows, width), bf16), pltpu.SemaphoreType.DMA(())),
        flops=10**9,
        data=2**20,
        far=(1,),
    )
    *slot_parts, recv = lax.optimization_barrier((*slot_parts, recv))
    back = [along_y(slot_parts[shift], shift) for shift in (1, 2, 3)]
    aways = value_part((2, 1, 3), recv)
    slot_grad = (slot_parts[0] + back[0]) + (back[1] + back[2])
    slot_grad, recv, *aways = lax.optimization_barrier((slot_grad, recv, *aways))
    two_away, one_away, three_away = aways

    one, two, three = (swap(slot_grad, mask, mem_count) for mask in (1, 2, 3))
    slot_grad = (slot_grad + one) + (two + three)
    slot_grad, two_away, one_away = lax.optimization_barrier((slot_grad, two_away, one_away))
    step = swap(slot_grad, 4, mem_count)
    sums = [along_x(two_away, 2), along_x(one_away, 1)]
    slot_grad = slot_grad + step
    slot_grad, recv, three_away = lax.optimization_barrier((slot_grad, recv, three_away))
    step = swap(slot_grad, 12, mem_count)
    sums.append(along_x(three_away, 3))
    (mine,) = value_part((0,), recv)
    slot_grad = slot_grad + step

    own = subs // groups
    parts = run(
        part_kernel,
        shape((groups, 2 * own, width), bf16),
        (slot_grad, weights_t, picks_t, queries, sub_keys, layer_input),
        scratch=(
            pltpu.VMEM((2, slots, tokens), f32),
            pltpu.VMEM((slots, tokens), f32),
            pltpu.VMEM((slots, 16, tokens), bf16),
            pltpu.VMEM((slots, 16, tokens), bf16),
            pltpu.VMEM((halves, subs, tokens), bf16),
            pltpu.VMEM((tokens, queries.shape[1] // 4), bf16),
            pltpu.SemaphoreType.DMA(()),
        ),
        far=(3,),
    )
    parts, mine, *sums = lax.optimization_barrier((parts, mine, *sums))
    parts = lax.all_to_all(parts, "dp", 0, 0, tiled=True)
    key = run(functools.partial(sum_kernel, own), shape((own, width), bf16), (parts,))
    key, mine, *sums = lax.optimization_barrier((key, mine, *sums))
    others = [swap(key, mask, mem_count) for mask in (1, 2, 3)]
    proj_grad = run(
        functools.partial(sum_kernel, 0),
        shape((own, width), f32),
        (parts,),
        flops=10**9,
        data=2**19,
    )
    value_grad = run(
        add_kernel, shape((val_rows, width), f32), (mine, *sums), flops=10**9, data=2**19
    )
    key_grad = run(join_kernel, shape((halves, own, key_width), f32), (key, *others))
    return (value_grad, key_grad, proj_grad)


def solution(mesh):
    return jax.shard_map(
        step_body,
        mesh=mesh,
        in_specs=(
            P("dp", "mem"),
            P("dp", "mem"),
            P("dp", None),
            P("dp", None),
            P(None, "dp", None),
            P("dp", None),
            P(),
            P("dp", "mem"),
        ),
        out_specs=(P("dp", "mem"), P(None, "dp", None), P("dp", "mem")),
        check_vma=False,
    )
```

```python
import functools

import jax
import jax.numpy as jnp
from jax import lax
from jax.experimental import pallas as pl
from jax.experimental.pallas import tpu as pltpu
from jax.sharding import PartitionSpec as P


f32 = jnp.float32
bf16 = jnp.bfloat16
SIDE = 4
VM = pl.BlockSpec(memory_space=pltpu.VMEM)
FAR = pl.BlockSpec(memory_space=pltpu.HBM)


def run(kernel, outs, args, scratch=(), flops=0, data=0, far=()):
    return pl.pallas_call(
        kernel,
        out_shape=outs,
        in_specs=[FAR if at in far else VM for at in range(len(args))],
        out_specs=jax.tree.map(lambda _: VM, outs),
        scratch_shapes=list(scratch),
        cost_estimate=pl.CostEstimate(flops=flops, bytes_accessed=data, transcendentals=0),
        compiler_params=pltpu.CompilerParams(vmem_limit_bytes=16 * 2**20),
    )(*args)


def shape(dims, dtype):
    return jax.ShapeDtypeStruct(dims, dtype)


def row_codes(ids):
    power = ids >> 7
    scale = (1 << (power & 15)).astype(f32) * jnp.where(power >= 16, 65536.0, 1.0)
    return ((ids & 127) + 128).astype(f32) * scale


def pack_kernel(
    grad_ref, rows_ref, weights_ref, values_ref, out_ref, values_out_ref, ids_ref, wide_ref, sems
):
    tokens = grad_ref.shape[0]
    copies = [
        pltpu.make_async_copy(rows_ref, ids_ref, sems.at[0]),
        pltpu.make_async_copy(weights_ref, wide_ref, sems.at[1]),
        pltpu.make_async_copy(grad_ref, out_ref.at[pl.ds(0, tokens), :], sems.at[2]),
        pltpu.make_async_copy(values_ref, values_out_ref, sems.at[3]),
    ]
    for copy in copies:
        copy.start()
    copies[0].wait()
    copies[1].wait()
    both = jnp.concatenate([row_codes(ids_ref[...]), wide_ref[...]], axis=1)
    out_ref[tokens:, :] = both.astype(bf16)
    copies[2].wait()
    copies[3].wait()


def power_of(base, exponent, bits):
    scale = jnp.float32(1.0)
    for bit in range(bits):
        scale = scale * jnp.where((exponent >> bit) & 1 == 1, base ** (2**bit), 1.0)
    return scale


def group_rows(codes):
    row = lax.axis_index("dp") // SIDE
    moved = codes.astype(f32) * power_of(2.0**-8, row, 2)
    inside = (moved >= 128.0) & (moved < 32768.0)
    local = jnp.full(codes.shape, -128, jnp.int32)
    for step in (4, 2, 1):
        above = moved >= 128.0 * 2.0**step
        moved = jnp.where(above, moved * 2.0**-step, moved)
        local = jnp.where(above, local + 128 * step, local)
    return jnp.where(inside, local + moved.astype(jnp.int32), -1)


def slot_kernel(*refs):
    block_refs, values_refs, out_refs = refs[:SIDE], refs[SIDE : 2 * SIDE], refs[2 * SIDE :]
    slots, tokens = out_refs[0].shape
    val_rows = values_refs[0].shape[0]
    column = lax.axis_index("dp") % SIDE
    for back, block_ref in enumerate(block_refs):
        local = group_rows(block_ref[tokens:, :tokens])
        accs = [jnp.zeros((8, tokens), f32) for _ in range(slots // 8)]
        for shift, values_ref in enumerate(values_refs):
            score = lax.dot_general(
                values_ref[...],
                block_ref[:tokens, :],
                (((1,), (1,)), ((), ())),
                preferred_element_type=f32,
            )
            first = ((column + SIDE - shift) % SIDE) * (val_rows // 8)
            for part in range(slots // 8):
                rows = local[part * 8 : part * 8 + 8]
                low, high = rows & 7, (rows >> 3) - first
                for tile in range(val_rows // 8):
                    got = jnp.take_along_axis(score[tile * 8 : tile * 8 + 8], low, axis=0)
                    accs[part] = jnp.where(high == tile, got, accs[part])
        for part in range(slots // 8):
            out_refs[(SIDE - back) % SIDE][part * 8 : part * 8 + 8, :] = accs[part]


def wide_row(ref, at):
    return jnp.broadcast_to(ref[at, :][None, :], (16, ref.shape[1])).astype(bf16)


def value_kernel(shifts, *refs):
    block_refs, out_refs = refs[:SIDE], refs[SIDE:-4]
    rows_ref, wide_ref, bag_ref, grads_ref = refs[-4:]
    val_rows = out_refs[0].shape[0]
    slots, tokens = rows_ref.shape[1:]
    tiles = val_rows // 16
    owner = lax.axis_index("dp")
    row, column = owner // SIDE, owner % SIDE
    base = row_codes(lax.broadcasted_iota(jnp.int32, (val_rows, tokens), 0))
    for at, block_ref in enumerate(block_refs):
        rows_ref[at] = block_ref[tokens:, :tokens].astype(f32)
        wide_ref[at] = block_ref[tokens:, tokens:].astype(f32)
        grads_ref[at * tokens : at * tokens + tokens, :] = block_ref[:tokens, :]
    for shift, out_ref in zip(shifts, out_refs):
        holder = row * SIDE + (column + shift) % SIDE
        codes = (base * power_of(4.0, holder, 4)).astype(bf16)
        codes = [codes[tile * 16 : tile * 16 + 16] for tile in range(tiles)]

        def one(at, carry, codes=codes):
            span = pl.ds(pl.multiple_of(at * tokens, tokens), tokens)
            bags = [jnp.zeros((16, tokens), bf16)] * tiles
            for slot in range(slots):
                code_now = wide_row(rows_ref.at[at], slot)
                weight = wide_row(wide_ref.at[at], slot)
                bags = [jnp.where(code == code_now, weight, bag) for code, bag in zip(codes, bags)]
            for tile in range(tiles):
                bag_ref[tile * 16 : tile * 16 + 16, span] = bags[tile]
            return carry

        lax.fori_loop(0, SIDE, one, 0)
        total = jnp.dot(bag_ref[...], grads_ref[...], preferred_element_type=f32)
        out_ref[...] = total.astype(out_ref.dtype)


def add_kernel(*refs):
    total = refs[0][...].astype(f32)
    for ref in refs[1:-1]:
        total = total + ref[...].astype(f32)
    refs[-1][...] = total


def part_kernel(
    slot_ref,
    weights_ref,
    picks_ref,
    queries_ref,
    keys_ref,
    layer_ref,
    out_ref,
    score_ref,
    pick_code_ref,
    pick_wide_ref,
    score_wide_ref,
    sub_ref,
    mine_ref,
    sem,
):
    slots, tokens = slot_ref.shape
    halves, subs, width = keys_ref.shape
    quarter = lax.axis_index("mem") & 3
    cut = mine_ref.shape[1]
    fetch = pltpu.make_async_copy(
        queries_ref.at[:, pl.ds(pl.multiple_of(quarter * cut, cut), cut)], mine_ref, sem
    )
    fetch.start()
    weights = weights_ref[...]
    slot_grad = slot_ref[...]
    centered = slot_grad - jnp.sum(weights * slot_grad, axis=0, keepdims=True)
    score_ref[0] = weights * centered
    block = 128
    tiles = block // 16
    base = lax.broadcasted_iota(jnp.int32, (block, tokens), 0).astype(f32) + 128.0
    for half in range(halves):
        picks = picks_ref[half]
        merged = jnp.zeros((slots, tokens), f32)
        for slot in range(slots):
            same = picks == picks_ref[half, slot : slot + 1, :]
            merged = merged + jnp.where(same, score_ref[0, slot : slot + 1, :], 0.0)
        score_ref[1] = merged
        pick_code_ref[...] = row_codes(picks)
        for slot in range(slots):
            pick_wide_ref[slot] = wide_row(pick_code_ref, slot)
            score_wide_ref[slot] = wide_row(score_ref.at[1], slot)

        def one(at, carry, half=half):
            codes = (base * (1 << at).astype(f32)).astype(bf16)
            codes = [codes[tile * 16 : tile * 16 + 16] for tile in range(tiles)]
            accs = [jnp.zeros((16, tokens), bf16)] * tiles
            for slot in range(slots):
                pick, score = pick_wide_ref[slot], score_wide_ref[slot]
                accs = [jnp.where(code == pick, score, acc) for code, acc in zip(codes, accs)]
            for tile in range(tiles):
                start = pl.multiple_of(at * block + tile * 16, 16)
                sub_ref[half, pl.ds(start, 16), :] = accs[tile]
            return carry

        lax.fori_loop(0, subs // block, one, 0)
    dests = out_ref.shape[0]
    own = subs // dests
    layer = layer_ref[...]
    for half in range(halves):
        dquery = lax.dot_general(
            sub_ref[half], keys_ref[half], (((0,), (0,)), ((), ())), preferred_element_type=f32
        ).astype(bf16)
        proj = lax.dot_general(
            dquery, layer, (((0,), (0,)), ((), ())), preferred_element_type=f32
        ).astype(bf16)
        per = width // own
        for at in range(per):
            out_ref[half * per + at, :own, :] = proj[at * own : at * own + own]
    fetch.wait()
    key = jnp.dot(sub_ref[quarter >> 1], mine_ref[...], preferred_element_type=f32).astype(bf16)
    for at in range(dests):
        out_ref[at, own:, :] = key[at * own : at * own + own]


def sum_kernel(first, parts_ref, out_ref):
    rows = slice(first, first + out_ref.shape[0])
    total = parts_ref[0, rows, :].astype(f32)
    for at in range(1, parts_ref.shape[0]):
        total = total + parts_ref[at, rows, :].astype(f32)
    out_ref[...] = total.astype(out_ref.dtype)


def join_kernel(own_ref, one_ref, two_ref, three_ref, out_ref):
    quarter = lax.axis_index("mem") & 3
    cut = own_ref.shape[1]
    for at, ref in enumerate((own_ref, one_ref, two_ref, three_ref)):
        there = quarter ^ at
        out_ref[there >> 1, :, pl.ds(pl.multiple_of((there & 1) * cut, cut), cut)] = ref[...].astype(f32)


def stay(x):
    return pltpu.with_memory_space_constraint(x, pltpu.HBM)


def swap(x, mask, count):
    return lax.ppermute(x, "mem", [(at, at ^ mask) for at in range(count)])


def step_body(grad_out, values, slot_rows, weights, sub_picks, queries, sub_keys, layer_input):
    groups = lax.axis_size("dp")
    mem_count = lax.axis_size("mem")
    tokens, width = grad_out.shape
    slots = slot_rows.shape[1]
    val_rows = values.shape[0]
    halves, subs, key_width = sub_keys.shape
    weights_t = weights.T
    rows_t = slot_rows.T
    picks_t = jnp.swapaxes(sub_picks, 1, 2)

    def along_x(x, shift):
        return lax.ppermute(
            x, "dp", [(at, at // SIDE * SIDE + (at + shift) % SIDE) for at in range(groups)]
        )

    def along_y(x, shift):
        return lax.ppermute(x, "dp", [(at, (at + shift * SIDE) % groups) for at in range(groups)])

    far_values = along_x(values, 2)
    sent, own_values = run(
        pack_kernel,
        [shape((tokens + slots, width), bf16), shape(values.shape, bf16)],
        [stay(x) for x in (grad_out, rows_t, weights_t, values)],
        scratch=(
            pltpu.VMEM((slots, tokens), jnp.int32),
            pltpu.VMEM((slots, tokens), f32),
            pltpu.SemaphoreType.DMA((4,)),
        ),
        far=(0, 1, 2, 3),
    )
    recv = [sent] + [along_y(sent, shift) for shift in (1, 2, 3)]
    all_values = [own_values, along_x(values, 1), far_values, along_x(values, 3)]

    def value_part(shifts, recv):
        return run(
            functools.partial(value_kernel, shifts),
            [shape((val_rows, width), bf16 if shift else f32) for shift in shifts],
            recv,
            scratch=(
                pltpu.VMEM((SIDE, slots, tokens), f32),
                pltpu.VMEM((SIDE, slots, tokens), f32),
                pltpu.VMEM((val_rows, SIDE * tokens), bf16),
                pltpu.VMEM((SIDE * tokens, width), bf16),
            ),
            flops=2 * 10**9,
            data=2**20,
        )

    slot_parts = run(
        slot_kernel,
        [shape((slots, tokens), f32)] * SIDE,
        (*recv, *all_values),
        flops=10**9,
        data=2**20,
    )
    slot_parts, recv = lax.optimization_barrier((slot_parts, recv))
    back = [along_y(slot_parts[shift], shift) for shift in (1, 2, 3)]
    aways = value_part((2, 1, 3), recv)
    slot_grad = (slot_parts[0] + back[0]) + (back[1] + back[2])
    slot_grad, recv, aways = lax.optimization_barrier((slot_grad, recv, aways))
    two_away, one_away, three_away = aways

    one, two, three = (swap(slot_grad, mask, mem_count) for mask in (1, 2, 3))
    slot_grad = (slot_grad + one) + (two + three)
    slot_grad, two_away, one_away = lax.optimization_barrier((slot_grad, two_away, one_away))
    step = swap(slot_grad, 4, mem_count)
    sums = [along_x(two_away, 2), along_x(one_away, 1)]
    slot_grad = slot_grad + step
    slot_grad, recv, three_away = lax.optimization_barrier((slot_grad, recv, three_away))
    step = swap(slot_grad, 12, mem_count)
    sums.append(along_x(three_away, 3))
    (mine,) = value_part((0,), recv)
    slot_grad = slot_grad + step

    own = subs // groups
    parts = run(
        part_kernel,
        shape((groups, 2 * own, width), bf16),
        (slot_grad, weights_t, picks_t, queries, sub_keys, layer_input),
        scratch=(
            pltpu.VMEM((2, slots, tokens), f32),
            pltpu.VMEM((slots, tokens), f32),
            pltpu.VMEM((slots, 16, tokens), bf16),
            pltpu.VMEM((slots, 16, tokens), bf16),
            pltpu.VMEM((halves, subs, tokens), bf16),
            pltpu.VMEM((tokens, queries.shape[1] // 4), bf16),
            pltpu.SemaphoreType.DMA(()),
        ),
        far=(3,),
    )
    parts, mine, *sums = lax.optimization_barrier((parts, mine, *sums))
    parts = lax.all_to_all(parts, "dp", 0, 0, tiled=True)
    key = run(functools.partial(sum_kernel, own), shape((own, width), bf16), (parts,))
    key, mine, *sums = lax.optimization_barrier((key, mine, *sums))
    others = [swap(key, mask, mem_count) for mask in (1, 2, 3)]
    proj_grad = run(
        functools.partial(sum_kernel, 0),
        shape((own, width), f32),
        (parts,),
        flops=10**9,
        data=2**19,
    )
    value_grad = run(
        add_kernel, shape((val_rows, width), f32), (mine, *sums), flops=10**9, data=2**19
    )
    key_grad = run(join_kernel, shape((halves, own, key_width), f32), (key, *others))
    return (value_grad, key_grad, proj_grad)


def solution(mesh):
    return jax.shard_map(
        step_body,
        mesh=mesh,
        in_specs=(
            P("dp", "mem"),
            P("dp", "mem"),
            P("dp", None),
            P("dp", None),
            P(None, "dp", None),
            P("dp", None),
            P(),
            P("dp", "mem"),
        ),
        out_specs=(P("dp", "mem"), P(None, "dp", None), P("dp", "mem")),
        check_vma=False,
    )
```

```python
import functools

import jax
import jax.numpy as jnp
from jax import lax
from jax.experimental import pallas as pl
from jax.experimental.pallas import tpu as pltpu
from jax.sharding import PartitionSpec as P


f32 = jnp.float32
bf16 = jnp.bfloat16
SIDE = 4
VM = pl.BlockSpec(memory_space=pltpu.VMEM)
FAR = pl.BlockSpec(memory_space=pltpu.HBM)


def run(kernel, outs, args, scratch=(), flops=0, data=0, far=()):
    return pl.pallas_call(
        kernel,
        out_shape=outs,
        in_specs=[FAR if at in far else VM for at in range(len(args))],
        out_specs=jax.tree.map(lambda _: VM, outs),
        scratch_shapes=list(scratch),
        cost_estimate=pl.CostEstimate(flops=flops, bytes_accessed=data, transcendentals=0),
        compiler_params=pltpu.CompilerParams(vmem_limit_bytes=16 * 2**20),
    )(*args)


def shape(dims, dtype):
    return jax.ShapeDtypeStruct(dims, dtype)


def row_codes(ids):
    power = ids >> 7
    scale = (1 << (power & 15)).astype(f32) * jnp.where(power >= 16, 65536.0, 1.0)
    return ((ids & 127) + 128).astype(f32) * scale


def pack_kernel(
    grad_ref, rows_ref, weights_ref, values_ref, out_ref, values_out_ref, ids_ref, wide_ref, sems
):
    tokens = grad_ref.shape[0]
    copies = [
        pltpu.make_async_copy(rows_ref, ids_ref, sems.at[0]),
        pltpu.make_async_copy(weights_ref, wide_ref, sems.at[1]),
        pltpu.make_async_copy(grad_ref, out_ref.at[pl.ds(0, tokens), :], sems.at[2]),
        pltpu.make_async_copy(values_ref, values_out_ref, sems.at[3]),
    ]
    for copy in copies:
        copy.start()
    copies[0].wait()
    copies[1].wait()
    both = jnp.concatenate([row_codes(ids_ref[...]), wide_ref[...]], axis=1)
    out_ref[tokens:, :] = both.astype(bf16)
    copies[2].wait()
    copies[3].wait()


def power_of(base, exponent, bits):
    scale = jnp.float32(1.0)
    for bit in range(bits):
        scale = scale * jnp.where((exponent >> bit) & 1 == 1, base ** (2**bit), 1.0)
    return scale


def group_rows(codes):
    row = lax.axis_index("dp") // SIDE
    moved = codes.astype(f32) * power_of(2.0**-8, row, 2)
    inside = (moved >= 128.0) & (moved < 32768.0)
    local = jnp.full(codes.shape, -128, jnp.int32)
    for step in (4, 2, 1):
        above = moved >= 128.0 * 2.0**step
        moved = jnp.where(above, moved * 2.0**-step, moved)
        local = jnp.where(above, local + 128 * step, local)
    return jnp.where(inside, local + moved.astype(jnp.int32), -1)


def slot_kernel(*refs):
    block_refs, values_refs, out_refs = refs[:SIDE], refs[SIDE : 2 * SIDE], refs[2 * SIDE :]
    slots, tokens = out_refs[0].shape
    val_rows = values_refs[0].shape[0]
    column = lax.axis_index("dp") % SIDE
    for back, block_ref in enumerate(block_refs):
        local = group_rows(block_ref[tokens:, :tokens])
        accs = [jnp.zeros((8, tokens), f32) for _ in range(slots // 8)]
        for shift, values_ref in enumerate(values_refs):
            score = lax.dot_general(
                values_ref[...],
                block_ref[:tokens, :],
                (((1,), (1,)), ((), ())),
                preferred_element_type=f32,
            )
            first = ((column + SIDE - shift) % SIDE) * (val_rows // 8)
            for part in range(slots // 8):
                rows = local[part * 8 : part * 8 + 8]
                low, high = rows & 7, (rows >> 3) - first
                for tile in range(val_rows // 8):
                    got = jnp.take_along_axis(score[tile * 8 : tile * 8 + 8], low, axis=0)
                    accs[part] = jnp.where(high == tile, got, accs[part])
        for part in range(slots // 8):
            out_refs[(SIDE - back) % SIDE][part * 8 : part * 8 + 8, :] = accs[part]


def wide_row(ref, at):
    return jnp.broadcast_to(ref[at, :][None, :], (16, ref.shape[1])).astype(bf16)


def value_kernel(shifts, *refs):
    block_refs, out_refs = refs[:SIDE], refs[SIDE:-4]
    rows_ref, wide_ref, bag_ref, grads_ref = refs[-4:]
    val_rows = out_refs[0].shape[0]
    slots, tokens = rows_ref.shape[1:]
    tiles = val_rows // 16
    owner = lax.axis_index("dp")
    row, column = owner // SIDE, owner % SIDE
    base = row_codes(lax.broadcasted_iota(jnp.int32, (val_rows, tokens), 0))
    for at, block_ref in enumerate(block_refs):
        rows_ref[at] = block_ref[tokens:, :tokens].astype(f32)
        wide_ref[at] = block_ref[tokens:, tokens:].astype(f32)
        grads_ref[at * tokens : at * tokens + tokens, :] = block_ref[:tokens, :]
    for shift, out_ref in zip(shifts, out_refs):
        holder = row * SIDE + (column + shift) % SIDE
        codes = (base * power_of(4.0, holder, 4)).astype(bf16)
        codes = [codes[tile * 16 : tile * 16 + 16] for tile in range(tiles)]

        def one(at, carry, codes=codes):
            span = pl.ds(pl.multiple_of(at * tokens, tokens), tokens)
            bags = [jnp.zeros((16, tokens), bf16)] * tiles
            for slot in range(slots):
                code_now = wide_row(rows_ref.at[at], slot)
                weight = wide_row(wide_ref.at[at], slot)
                bags = [jnp.where(code == code_now, weight, bag) for code, bag in zip(codes, bags)]
            for tile in range(tiles):
                bag_ref[tile * 16 : tile * 16 + 16, span] = bags[tile]
            return carry

        lax.fori_loop(0, SIDE, one, 0)
        total = jnp.dot(bag_ref[...], grads_ref[...], preferred_element_type=f32)
        out_ref[...] = total.astype(out_ref.dtype)


def add_kernel(*refs):
    total = refs[0][...].astype(f32)
    for ref in refs[1:-1]:
        total = total + ref[...].astype(f32)
    refs[-1][...] = total


def part_kernel(
    slot_ref,
    weights_ref,
    picks_ref,
    queries_ref,
    keys_ref,
    layer_ref,
    out_ref,
    score_ref,
    pick_code_ref,
    pick_wide_ref,
    score_wide_ref,
    sub_ref,
    mine_ref,
    sem,
):
    slots, tokens = slot_ref.shape
    _, subs, width = keys_ref.shape
    quarter = lax.axis_index("mem") & 3
    cut = mine_ref.shape[1]
    fetch = pltpu.make_async_copy(
        queries_ref.at[:, pl.ds(pl.multiple_of(quarter * cut, cut), cut)], mine_ref, sem
    )
    fetch.start()
    weights = weights_ref[...]
    slot_grad = slot_ref[...]
    centered = slot_grad - jnp.sum(weights * slot_grad, axis=0, keepdims=True)
    score_ref[0] = weights * centered
    block = 128
    tiles = block // 16
    base = lax.broadcasted_iota(jnp.int32, (block, tokens), 0).astype(f32) + 128.0
    dests = out_ref.shape[0]
    own = subs // dests
    per = width // own
    layer = layer_ref[...]

    def spread(half):
        picks = picks_ref[half]
        merged = jnp.zeros((slots, tokens), f32)
        for slot in range(slots):
            same = picks == picks_ref[half, slot : slot + 1, :]
            merged = merged + jnp.where(same, score_ref[0, slot : slot + 1, :], 0.0)
        score_ref[1] = merged
        pick_code_ref[...] = row_codes(picks)
        for slot in range(slots):
            pick_wide_ref[half, slot] = wide_row(pick_code_ref, slot)
            score_wide_ref[half, slot] = wide_row(score_ref.at[1], slot)

    def build(half, at, scale):
        codes = (base * scale).astype(bf16)
        codes = [codes[tile * 16 : tile * 16 + 16] for tile in range(tiles)]
        accs = [jnp.zeros((16, tokens), bf16)] * tiles
        for slot in range(slots):
            pick, score = pick_wide_ref[half, slot], score_wide_ref[half, slot]
            accs = [jnp.where(code == pick, score, acc) for code, acc in zip(codes, accs)]
        for tile in range(tiles):
            start = at * block + tile * 16
            if not isinstance(at, int):
                start = pl.multiple_of(start, 16)
            sub_ref[half, pl.ds(start, 16), :] = accs[tile]

    def multiply(half):
        dquery = lax.dot_general(
            sub_ref[half], keys_ref[half], (((0,), (0,)), ((), ())), preferred_element_type=f32
        ).astype(bf16)
        proj = lax.dot_general(
            dquery, layer, (((0,), (0,)), ((), ())), preferred_element_type=f32
        ).astype(bf16)
        for at in range(per):
            out_ref[half * per + at, :own, :] = proj[at * own : at * own + own]

    def one(at, carry):
        build(0, at, (1 << at).astype(f32))
        return carry

    spread(0)
    lax.fori_loop(0, subs // block, one, 0)
    spread(1)
    multiply(0)
    for at in range(subs // block):
        build(1, at, 2.0**at)
    multiply(1)
    fetch.wait()
    key = jnp.dot(sub_ref[quarter >> 1], mine_ref[...], preferred_element_type=f32).astype(bf16)
    for at in range(dests):
        out_ref[at, own:, :] = key[at * own : at * own + own]


def sum_kernel(first, parts_ref, out_ref):
    rows = slice(first, first + out_ref.shape[0])
    total = parts_ref[0, rows, :].astype(f32)
    for at in range(1, parts_ref.shape[0]):
        total = total + parts_ref[at, rows, :].astype(f32)
    out_ref[...] = total.astype(out_ref.dtype)


def join_kernel(own_ref, one_ref, two_ref, three_ref, out_ref):
    quarter = lax.axis_index("mem") & 3
    cut = own_ref.shape[1]
    for at, ref in enumerate((own_ref, one_ref, two_ref, three_ref)):
        there = quarter ^ at
        out_ref[there >> 1, :, pl.ds(pl.multiple_of((there & 1) * cut, cut), cut)] = ref[...].astype(f32)


def stay(x):
    return pltpu.with_memory_space_constraint(x, pltpu.HBM)


def swap(x, mask, count):
    return lax.ppermute(x, "mem", [(at, at ^ mask) for at in range(count)])


def step_body(grad_out, values, slot_rows, weights, sub_picks, queries, sub_keys, layer_input):
    groups = lax.axis_size("dp")
    mem_count = lax.axis_size("mem")
    tokens, width = grad_out.shape
    slots = slot_rows.shape[1]
    val_rows = values.shape[0]
    halves, subs, key_width = sub_keys.shape
    weights_t = weights.T
    rows_t = slot_rows.T
    picks_t = jnp.swapaxes(sub_picks, 1, 2)

    def along_x(x, shift):
        return lax.ppermute(
            x, "dp", [(at, at // SIDE * SIDE + (at + shift) % SIDE) for at in range(groups)]
        )

    def along_y(x, shift):
        return lax.ppermute(x, "dp", [(at, (at + shift * SIDE) % groups) for at in range(groups)])

    far_values = along_x(values, 2)
    sent, own_values = run(
        pack_kernel,
        [shape((tokens + slots, width), bf16), shape(values.shape, bf16)],
        [stay(x) for x in (grad_out, rows_t, weights_t, values)],
        scratch=(
            pltpu.VMEM((slots, tokens), jnp.int32),
            pltpu.VMEM((slots, tokens), f32),
            pltpu.SemaphoreType.DMA((4,)),
        ),
        far=(0, 1, 2, 3),
    )
    recv = [sent] + [along_y(sent, shift) for shift in (1, 2, 3)]
    all_values = [own_values, along_x(values, 1), far_values, along_x(values, 3)]

    def value_part(shifts, recv):
        return run(
            functools.partial(value_kernel, shifts),
            [shape((val_rows, width), bf16 if shift else f32) for shift in shifts],
            recv,
            scratch=(
                pltpu.VMEM((SIDE, slots, tokens), f32),
                pltpu.VMEM((SIDE, slots, tokens), f32),
                pltpu.VMEM((val_rows, SIDE * tokens), bf16),
                pltpu.VMEM((SIDE * tokens, width), bf16),
            ),
            flops=2 * 10**9,
            data=2**20,
        )

    slot_parts = run(
        slot_kernel,
        [shape((slots, tokens), f32)] * SIDE,
        (*recv, *all_values),
        flops=10**9,
        data=2**20,
    )
    slot_parts, recv = lax.optimization_barrier((slot_parts, recv))
    back = [along_y(slot_parts[shift], shift) for shift in (1, 2, 3)]
    aways = value_part((2, 1, 3), recv)
    slot_grad = (slot_parts[0] + back[0]) + (back[1] + back[2])
    slot_grad, recv, aways = lax.optimization_barrier((slot_grad, recv, aways))
    two_away, one_away, three_away = aways

    one, two, three = (swap(slot_grad, mask, mem_count) for mask in (1, 2, 3))
    sums = [along_x(two_away, 2)]
    slot_grad = (slot_grad + one) + (two + three)
    slot_grad, one_away = lax.optimization_barrier((slot_grad, one_away))
    step = swap(slot_grad, 4, mem_count)
    sums.append(along_x(one_away, 1))
    slot_grad = slot_grad + step
    slot_grad, recv, three_away = lax.optimization_barrier((slot_grad, recv, three_away))
    step = swap(slot_grad, 12, mem_count)
    sums.append(along_x(three_away, 3))
    (mine,) = value_part((0,), recv)
    slot_grad = slot_grad + step

    own = subs // groups
    parts = run(
        part_kernel,
        shape((groups, 2 * own, width), bf16),
        (slot_grad, weights_t, picks_t, queries, sub_keys, layer_input),
        scratch=(
            pltpu.VMEM((2, slots, tokens), f32),
            pltpu.VMEM((slots, tokens), f32),
            pltpu.VMEM((halves, slots, 16, tokens), bf16),
            pltpu.VMEM((halves, slots, 16, tokens), bf16),
            pltpu.VMEM((halves, subs, tokens), bf16),
            pltpu.VMEM((tokens, queries.shape[1] // 4), bf16),
            pltpu.SemaphoreType.DMA(()),
        ),
        far=(3,),
    )
    parts, mine, *sums = lax.optimization_barrier((parts, mine, *sums))
    parts = lax.all_to_all(parts, "dp", 0, 0, tiled=True)
    key = run(functools.partial(sum_kernel, own), shape((own, width), bf16), (parts,))
    key, mine, *sums = lax.optimization_barrier((key, mine, *sums))
    others = [swap(key, mask, mem_count) for mask in (1, 2, 3)]
    proj_grad = run(
        functools.partial(sum_kernel, 0),
        shape((own, width), f32),
        (parts,),
        flops=10**9,
        data=2**19,
    )
    value_grad = run(
        add_kernel, shape((val_rows, width), f32), (mine, *sums), flops=10**9, data=2**19
    )
    key_grad = run(join_kernel, shape((halves, own, key_width), f32), (key, *others))
    return (value_grad, key_grad, proj_grad)


def solution(mesh):
    return jax.shard_map(
        step_body,
        mesh=mesh,
        in_specs=(
            P("dp", "mem"),
            P("dp", "mem"),
            P("dp", None),
            P("dp", None),
            P(None, "dp", None),
            P("dp", None),
            P(),
            P("dp", "mem"),
        ),
        out_specs=(P("dp", "mem"), P(None, "dp", None), P("dp", "mem")),
        check_vma=False,
    )
```

```python
import functools

import jax
import jax.numpy as jnp
from jax import lax
from jax.experimental import pallas as pl
from jax.experimental.pallas import tpu as pltpu
from jax.sharding import PartitionSpec as P


f32 = jnp.float32
bf16 = jnp.bfloat16
SIDE = 4
VM = pl.BlockSpec(memory_space=pltpu.VMEM)
FAR = pl.BlockSpec(memory_space=pltpu.HBM)


def run(kernel, outs, args, scratch=(), flops=0, data=0, far=()):
    return pl.pallas_call(
        kernel,
        out_shape=outs,
        in_specs=[FAR if at in far else VM for at in range(len(args))],
        out_specs=jax.tree.map(lambda _: VM, outs),
        scratch_shapes=list(scratch),
        cost_estimate=pl.CostEstimate(flops=flops, bytes_accessed=data, transcendentals=0),
        compiler_params=pltpu.CompilerParams(vmem_limit_bytes=16 * 2**20),
    )(*args)


def shape(dims, dtype):
    return jax.ShapeDtypeStruct(dims, dtype)


def row_codes(ids):
    power = ids >> 7
    scale = (1 << (power & 15)).astype(f32) * jnp.where(power >= 16, 65536.0, 1.0)
    return ((ids & 127) + 128).astype(f32) * scale


def pack_kernel(
    grad_ref, rows_ref, weights_ref, values_ref, out_ref, values_out_ref, ids_ref, wide_ref, sems
):
    tokens = grad_ref.shape[0]
    copies = [
        pltpu.make_async_copy(rows_ref, ids_ref, sems.at[0]),
        pltpu.make_async_copy(weights_ref, wide_ref, sems.at[1]),
        pltpu.make_async_copy(grad_ref, out_ref.at[pl.ds(0, tokens), :], sems.at[2]),
        pltpu.make_async_copy(values_ref, values_out_ref, sems.at[3]),
    ]
    for copy in copies:
        copy.start()
    copies[0].wait()
    copies[1].wait()
    both = jnp.concatenate([row_codes(ids_ref[...]), wide_ref[...]], axis=1)
    out_ref[tokens:, :] = both.astype(bf16)
    copies[2].wait()
    copies[3].wait()


def power_of(base, exponent, bits):
    scale = jnp.float32(1.0)
    for bit in range(bits):
        scale = scale * jnp.where((exponent >> bit) & 1 == 1, base ** (2**bit), 1.0)
    return scale


def group_rows(codes):
    row = lax.axis_index("dp") // SIDE
    moved = codes.astype(f32) * power_of(2.0**-8, row, 2)
    inside = (moved >= 128.0) & (moved < 32768.0)
    local = jnp.full(codes.shape, -128, jnp.int32)
    for step in (4, 2, 1):
        above = moved >= 128.0 * 2.0**step
        moved = jnp.where(above, moved * 2.0**-step, moved)
        local = jnp.where(above, local + 128 * step, local)
    return jnp.where(inside, local + moved.astype(jnp.int32), -1)


def slot_kernel(*refs):
    block_refs, values_refs, out_refs = refs[:SIDE], refs[SIDE : 2 * SIDE], refs[2 * SIDE :]
    slots, tokens = out_refs[0].shape
    val_rows = values_refs[0].shape[0]
    column = lax.axis_index("dp") % SIDE
    for back, block_ref in enumerate(block_refs):
        local = group_rows(block_ref[tokens:, :tokens])
        accs = [jnp.zeros((8, tokens), f32) for _ in range(slots // 8)]
        for shift, values_ref in enumerate(values_refs):
            score = lax.dot_general(
                values_ref[...],
                block_ref[:tokens, :],
                (((1,), (1,)), ((), ())),
                preferred_element_type=f32,
            )
            first = ((column + SIDE - shift) % SIDE) * (val_rows // 8)
            for part in range(slots // 8):
                rows = local[part * 8 : part * 8 + 8]
                low, high = rows & 7, (rows >> 3) - first
                for tile in range(val_rows // 8):
                    got = jnp.take_along_axis(score[tile * 8 : tile * 8 + 8], low, axis=0)
                    accs[part] = jnp.where(high == tile, got, accs[part])
        for part in range(slots // 8):
            out_refs[(SIDE - back) % SIDE][part * 8 : part * 8 + 8, :] = accs[part]


def wide_row(ref, at):
    return jnp.broadcast_to(ref[at, :][None, :], (16, ref.shape[1])).astype(bf16)


def value_kernel(shifts, *refs):
    block_refs, out_refs = refs[:SIDE], refs[SIDE:-4]
    rows_ref, wide_ref, bag_ref, grads_ref = refs[-4:]
    val_rows = out_refs[0].shape[0]
    slots, tokens = rows_ref.shape[1:]
    tiles = val_rows // 16
    owner = lax.axis_index("dp")
    row, column = owner // SIDE, owner % SIDE
    base = row_codes(lax.broadcasted_iota(jnp.int32, (val_rows, tokens), 0))
    for at, block_ref in enumerate(block_refs):
        rows_ref[at] = block_ref[tokens:, :tokens].astype(f32)
        wide_ref[at] = block_ref[tokens:, tokens:].astype(f32)
        grads_ref[at * tokens : at * tokens + tokens, :] = block_ref[:tokens, :]
    for shift, out_ref in zip(shifts, out_refs):
        holder = row * SIDE + (column + shift) % SIDE
        codes = (base * power_of(4.0, holder, 4)).astype(bf16)
        codes = [codes[tile * 16 : tile * 16 + 16] for tile in range(tiles)]

        def one(at, carry, codes=codes):
            span = pl.ds(pl.multiple_of(at * tokens, tokens), tokens)
            bags = [jnp.zeros((16, tokens), bf16)] * tiles
            for slot in range(slots):
                code_now = wide_row(rows_ref.at[at], slot)
                weight = wide_row(wide_ref.at[at], slot)
                bags = [jnp.where(code == code_now, weight, bag) for code, bag in zip(codes, bags)]
            for tile in range(tiles):
                bag_ref[tile * 16 : tile * 16 + 16, span] = bags[tile]
            return carry

        lax.fori_loop(0, SIDE, one, 0)
        total = jnp.dot(bag_ref[...], grads_ref[...], preferred_element_type=f32)
        out_ref[...] = total.astype(out_ref.dtype)


def add_kernel(*refs):
    total = refs[0][...].astype(f32)
    for ref in refs[1:-1]:
        total = total + ref[...].astype(f32)
    refs[-1][...] = total


def part_kernel(
    slot_ref,
    weights_ref,
    picks_ref,
    queries_ref,
    keys_ref,
    layer_ref,
    out_ref,
    score_ref,
    pick_code_ref,
    pick_wide_ref,
    score_wide_ref,
    sub_ref,
    mine_ref,
    sem,
):
    slots, tokens = slot_ref.shape
    _, subs, width = keys_ref.shape
    quarter = lax.axis_index("mem") & 3
    cut = mine_ref.shape[1]
    fetch = pltpu.make_async_copy(
        queries_ref.at[:, pl.ds(pl.multiple_of(quarter * cut, cut), cut)], mine_ref, sem
    )
    fetch.start()
    weights = weights_ref[...]
    slot_grad = slot_ref[...]
    centered = slot_grad - jnp.sum(weights * slot_grad, axis=0, keepdims=True)
    score_ref[0] = weights * centered
    block = 128
    tiles = block // 16
    base = lax.broadcasted_iota(jnp.int32, (block, tokens), 0).astype(f32) + 128.0
    dests = out_ref.shape[0]
    own = subs // dests
    per = width // own
    layer = layer_ref[...]

    def spread(half):
        picks = picks_ref[half]
        merged = jnp.zeros((slots, tokens), f32)
        for slot in range(slots):
            same = picks == picks_ref[half, slot : slot + 1, :]
            merged = merged + jnp.where(same, score_ref[0, slot : slot + 1, :], 0.0)
        score_ref[1] = merged
        pick_code_ref[...] = row_codes(picks)
        for slot in range(slots):
            pick_wide_ref[half, slot] = wide_row(pick_code_ref, slot)
            score_wide_ref[half, slot] = wide_row(score_ref.at[1], slot)

    def build(half, at, scale):
        codes = (base * scale).astype(bf16)
        codes = [codes[tile * 16 : tile * 16 + 16] for tile in range(tiles)]
        accs = [jnp.zeros((16, tokens), bf16)] * tiles
        for slot in range(slots):
            pick, score = pick_wide_ref[half, slot], score_wide_ref[half, slot]
            accs = [jnp.where(code == pick, score, acc) for code, acc in zip(codes, accs)]
        for tile in range(tiles):
            start = at * block + tile * 16
            if not isinstance(at, int):
                start = pl.multiple_of(start, 16)
            sub_ref[half, pl.ds(start, 16), :] = accs[tile]

    def multiply(half):
        dquery = lax.dot_general(
            sub_ref[half], keys_ref[half], (((0,), (0,)), ((), ())), preferred_element_type=f32
        ).astype(bf16)
        proj = lax.dot_general(
            dquery, layer, (((0,), (0,)), ((), ())), preferred_element_type=f32
        ).astype(bf16)
        for at in range(per):
            out_ref[half * per + at, :own, :] = proj[at * own : at * own + own]

    def one(at, carry):
        build(0, at, (1 << at).astype(f32))
        return carry

    spread(0)
    lax.fori_loop(0, subs // block, one, 0)
    spread(1)
    multiply(0)
    for at in range(subs // block):
        build(1, at, 2.0**at)
    multiply(1)
    fetch.wait()
    key = jnp.dot(sub_ref[quarter >> 1], mine_ref[...], preferred_element_type=f32).astype(bf16)
    for at in range(dests):
        out_ref[at, own:, :] = key[at * own : at * own + own]


def sum_kernel(first, parts_ref, out_ref):
    rows = slice(first, first + out_ref.shape[0])
    total = parts_ref[0, rows, :].astype(f32)
    for at in range(1, parts_ref.shape[0]):
        total = total + parts_ref[at, rows, :].astype(f32)
    out_ref[...] = total.astype(out_ref.dtype)


def join_kernel(own_ref, one_ref, two_ref, three_ref, out_ref):
    quarter = lax.axis_index("mem") & 3
    cut = own_ref.shape[1]
    for at, ref in enumerate((own_ref, one_ref, two_ref, three_ref)):
        there = quarter ^ at
        out_ref[there >> 1, :, pl.ds(pl.multiple_of((there & 1) * cut, cut), cut)] = ref[...].astype(f32)


def stay(x):
    return pltpu.with_memory_space_constraint(x, pltpu.HBM)


def swap(x, mask, count):
    return lax.ppermute(x, "mem", [(at, at ^ mask) for at in range(count)])


def step_body(grad_out, values, slot_rows, weights, sub_picks, queries, sub_keys, layer_input):
    groups = lax.axis_size("dp")
    mem_count = lax.axis_size("mem")
    tokens, width = grad_out.shape
    slots = slot_rows.shape[1]
    val_rows = values.shape[0]
    halves, subs, key_width = sub_keys.shape
    weights_t = weights.T
    rows_t = slot_rows.T
    picks_t = jnp.swapaxes(sub_picks, 1, 2)

    def along_x(x, shift):
        return lax.ppermute(
            x, "dp", [(at, at // SIDE * SIDE + (at + shift) % SIDE) for at in range(groups)]
        )

    def along_y(x, shift):
        return lax.ppermute(x, "dp", [(at, (at + shift * SIDE) % groups) for at in range(groups)])

    far_values = along_x(values, 2)
    sent, own_values = run(
        pack_kernel,
        [shape((tokens + slots, width), bf16), shape(values.shape, bf16)],
        [stay(x) for x in (grad_out, rows_t, weights_t, values)],
        scratch=(
            pltpu.VMEM((slots, tokens), jnp.int32),
            pltpu.VMEM((slots, tokens), f32),
            pltpu.SemaphoreType.DMA((4,)),
        ),
        far=(0, 1, 2, 3),
    )
    recv = [sent] + [along_y(sent, shift) for shift in (1, 2, 3)]
    all_values = [own_values, along_x(values, 1), far_values, along_x(values, 3)]

    def value_part(shifts, recv):
        return run(
            functools.partial(value_kernel, shifts),
            [shape((val_rows, width), bf16 if shift else f32) for shift in shifts],
            recv,
            scratch=(
                pltpu.VMEM((SIDE, slots, tokens), f32),
                pltpu.VMEM((SIDE, slots, tokens), f32),
                pltpu.VMEM((val_rows, SIDE * tokens), bf16),
                pltpu.VMEM((SIDE * tokens, width), bf16),
            ),
            flops=2 * 10**9,
            data=2**20,
        )

    two_away, one_away, three_away = value_part((2, 1, 3), recv)
    slot_parts = run(
        slot_kernel,
        [shape((slots, tokens), f32)] * SIDE,
        (*recv, *all_values),
        flops=10**9,
        data=2**20,
    )
    slot_parts, recv = lax.optimization_barrier((slot_parts, recv))
    back = [along_y(slot_parts[shift], shift) for shift in (1, 2, 3)]
    (mine,) = value_part((0,), recv)
    sums = [along_x(two_away, 2)]
    slot_grad = (slot_parts[0] + back[0]) + (back[1] + back[2])
    slot_grad, one_away, three_away, mine = lax.optimization_barrier(
        (slot_grad, one_away, three_away, mine)
    )

    one, two, three = (swap(slot_grad, mask, mem_count) for mask in (1, 2, 3))
    sums.append(along_x(one_away, 1))
    slot_grad = (slot_grad + one) + (two + three)
    slot_grad, three_away = lax.optimization_barrier((slot_grad, three_away))
    step = swap(slot_grad, 4, mem_count)
    sums.append(along_x(three_away, 3))
    slot_grad = slot_grad + step
    step = swap(slot_grad, 12, mem_count)
    slot_grad = slot_grad + step

    own = subs // groups
    parts = run(
        part_kernel,
        shape((groups, 2 * own, width), bf16),
        (slot_grad, weights_t, picks_t, queries, sub_keys, layer_input),
        scratch=(
            pltpu.VMEM((2, slots, tokens), f32),
            pltpu.VMEM((slots, tokens), f32),
            pltpu.VMEM((halves, slots, 16, tokens), bf16),
            pltpu.VMEM((halves, slots, 16, tokens), bf16),
            pltpu.VMEM((halves, subs, tokens), bf16),
            pltpu.VMEM((tokens, queries.shape[1] // 4), bf16),
            pltpu.SemaphoreType.DMA(()),
        ),
        far=(3,),
    )
    parts, mine, *sums = lax.optimization_barrier((parts, mine, *sums))
    parts = lax.all_to_all(parts, "dp", 0, 0, tiled=True)
    key = run(functools.partial(sum_kernel, own), shape((own, width), bf16), (parts,))
    key, mine, *sums = lax.optimization_barrier((key, mine, *sums))
    others = [swap(key, mask, mem_count) for mask in (1, 2, 3)]
    proj_grad = run(
        functools.partial(sum_kernel, 0),
        shape((own, width), f32),
        (parts,),
        flops=10**9,
        data=2**19,
    )
    value_grad = run(
        add_kernel, shape((val_rows, width), f32), (mine, *sums), flops=10**9, data=2**19
    )
    key_grad = run(join_kernel, shape((halves, own, key_width), f32), (key, *others))
    return (value_grad, key_grad, proj_grad)


def solution(mesh):
    return jax.shard_map(
        step_body,
        mesh=mesh,
        in_specs=(
            P("dp", "mem"),
            P("dp", "mem"),
            P("dp", None),
            P("dp", None),
            P(None, "dp", None),
            P("dp", None),
            P(),
            P("dp", "mem"),
        ),
        out_specs=(P("dp", "mem"), P(None, "dp", None), P("dp", "mem")),
        check_vma=False,
    )
```

```python
import functools

import jax
import jax.numpy as jnp
from jax import lax
from jax.experimental import pallas as pl
from jax.experimental.pallas import tpu as pltpu
from jax.sharding import PartitionSpec as P


f32 = jnp.float32
bf16 = jnp.bfloat16
SIDE = 4
VM = pl.BlockSpec(memory_space=pltpu.VMEM)
FAR = pl.BlockSpec(memory_space=pltpu.HBM)


def run(kernel, outs, args, scratch=(), flops=0, data=0, far=()):
    return pl.pallas_call(
        kernel,
        out_shape=outs,
        in_specs=[FAR if at in far else VM for at in range(len(args))],
        out_specs=jax.tree.map(lambda _: VM, outs),
        scratch_shapes=list(scratch),
        cost_estimate=pl.CostEstimate(flops=flops, bytes_accessed=data, transcendentals=0),
        compiler_params=pltpu.CompilerParams(vmem_limit_bytes=16 * 2**20),
    )(*args)


def shape(dims, dtype):
    return jax.ShapeDtypeStruct(dims, dtype)


def row_codes(ids):
    power = ids >> 7
    scale = (1 << (power & 15)).astype(f32) * jnp.where(power >= 16, 65536.0, 1.0)
    return ((ids & 127) + 128).astype(f32) * scale


def pack_kernel(
    grad_ref, rows_ref, weights_ref, values_ref, out_ref, values_out_ref, ids_ref, wide_ref, sems
):
    tokens = grad_ref.shape[0]
    copies = [
        pltpu.make_async_copy(rows_ref, ids_ref, sems.at[0]),
        pltpu.make_async_copy(weights_ref, wide_ref, sems.at[1]),
        pltpu.make_async_copy(grad_ref, out_ref.at[pl.ds(0, tokens), :], sems.at[2]),
        pltpu.make_async_copy(values_ref, values_out_ref, sems.at[3]),
    ]
    for copy in copies:
        copy.start()
    copies[0].wait()
    copies[1].wait()
    both = jnp.concatenate([row_codes(ids_ref[...]), wide_ref[...]], axis=1)
    out_ref[tokens:, :] = both.astype(bf16)
    copies[2].wait()
    copies[3].wait()


def power_of(base, exponent, bits):
    scale = jnp.float32(1.0)
    for bit in range(bits):
        scale = scale * jnp.where((exponent >> bit) & 1 == 1, base ** (2**bit), 1.0)
    return scale


def group_rows(codes):
    row = lax.axis_index("dp") // SIDE
    moved = codes.astype(f32) * power_of(2.0**-8, row, 2)
    inside = (moved >= 128.0) & (moved < 32768.0)
    local = jnp.full(codes.shape, -128, jnp.int32)
    for step in (4, 2, 1):
        above = moved >= 128.0 * 2.0**step
        moved = jnp.where(above, moved * 2.0**-step, moved)
        local = jnp.where(above, local + 128 * step, local)
    return jnp.where(inside, local + moved.astype(jnp.int32), -1)


def slot_kernel(*refs):
    block_refs, values_refs, out_refs = refs[:SIDE], refs[SIDE : 2 * SIDE], refs[2 * SIDE :]
    slots, tokens = out_refs[0].shape
    val_rows = values_refs[0].shape[0]
    column = lax.axis_index("dp") % SIDE
    for back, block_ref in enumerate(block_refs):
        local = group_rows(block_ref[tokens:, :tokens])
        accs = [jnp.zeros((8, tokens), f32) for _ in range(slots // 8)]
        for shift, values_ref in enumerate(values_refs):
            score = lax.dot_general(
                values_ref[...],
                block_ref[:tokens, :],
                (((1,), (1,)), ((), ())),
                preferred_element_type=f32,
            )
            first = ((column + SIDE - shift) % SIDE) * (val_rows // 8)
            for part in range(slots // 8):
                rows = local[part * 8 : part * 8 + 8]
                low, high = rows & 7, (rows >> 3) - first
                for tile in range(val_rows // 8):
                    got = jnp.take_along_axis(score[tile * 8 : tile * 8 + 8], low, axis=0)
                    accs[part] = jnp.where(high == tile, got, accs[part])
        for part in range(slots // 8):
            out_refs[(SIDE - back) % SIDE][part * 8 : part * 8 + 8, :] = accs[part]


def wide_row(ref, at):
    return jnp.broadcast_to(ref[at, :][None, :], (16, ref.shape[1])).astype(bf16)


def value_kernel(shifts, *refs):
    block_refs, out_refs = refs[:SIDE], refs[SIDE:-4]
    rows_ref, wide_ref, bag_ref, grads_ref = refs[-4:]
    val_rows = out_refs[0].shape[0]
    slots, tokens = rows_ref.shape[1:]
    tiles = val_rows // 16
    owner = lax.axis_index("dp")
    row, column = owner // SIDE, owner % SIDE
    base = row_codes(lax.broadcasted_iota(jnp.int32, (val_rows, tokens), 0))
    for at, block_ref in enumerate(block_refs):
        rows_ref[at] = block_ref[tokens:, :tokens].astype(f32)
        wide_ref[at] = block_ref[tokens:, tokens:].astype(f32)
        grads_ref[at * tokens : at * tokens + tokens, :] = block_ref[:tokens, :]
    for shift, out_ref in zip(shifts, out_refs):
        holder = row * SIDE + (column + shift) % SIDE
        codes = (base * power_of(4.0, holder, 4)).astype(bf16)
        codes = [codes[tile * 16 : tile * 16 + 16] for tile in range(tiles)]

        def one(at, carry, codes=codes):
            span = pl.ds(pl.multiple_of(at * tokens, tokens), tokens)
            bags = [jnp.zeros((16, tokens), bf16)] * tiles
            for slot in range(slots):
                code_now = wide_row(rows_ref.at[at], slot)
                weight = wide_row(wide_ref.at[at], slot)
                bags = [jnp.where(code == code_now, weight, bag) for code, bag in zip(codes, bags)]
            for tile in range(tiles):
                bag_ref[tile * 16 : tile * 16 + 16, span] = bags[tile]
            return carry

        lax.fori_loop(0, SIDE, one, 0)
        total = jnp.dot(bag_ref[...], grads_ref[...], preferred_element_type=f32)
        out_ref[...] = total.astype(out_ref.dtype)


def add_kernel(*refs):
    total = refs[0][...].astype(f32)
    for ref in refs[1:-1]:
        total = total + ref[...].astype(f32)
    refs[-1][...] = total


def find_kernel(picks_ref, out_ref, code_ref, wide_ref):
    halves, slots, tokens = picks_ref.shape
    subs = out_ref.shape[1]
    block = 128
    tiles = block // 16
    base = lax.broadcasted_iota(jnp.int32, (block, tokens), 0).astype(f32) + 128.0
    for half in range(halves):
        code_ref[...] = row_codes(picks_ref[half])
        for slot in range(slots):
            wide_ref[slot] = wide_row(code_ref, slot)

        def one(at, carry, half=half):
            codes = (base * (1 << at).astype(f32)).astype(bf16)
            codes = [codes[tile * 16 : tile * 16 + 16] for tile in range(tiles)]
            accs = [jnp.full((16, tokens), slots, bf16)] * tiles
            for slot in range(slots):
                pick = wide_ref[slot]
                this = jnp.full((16, tokens), slot, bf16)
                accs = [jnp.where(code == pick, this, acc) for code, acc in zip(codes, accs)]
            for tile in range(tiles):
                start = pl.multiple_of(at * block + tile * 16, 16)
                out_ref[half, pl.ds(start, 16), :] = accs[tile].astype(f32).astype(jnp.int32)
            return carry

        lax.fori_loop(0, subs // block, one, 0)


def part_kernel(
    slot_ref,
    weights_ref,
    picks_ref,
    found_ref,
    queries_ref,
    keys_ref,
    layer_ref,
    out_ref,
    score_ref,
    sub_ref,
    mine_ref,
    sem,
):
    slots, tokens = slot_ref.shape
    halves, subs, width = keys_ref.shape
    quarter = lax.axis_index("mem") & 3
    cut = mine_ref.shape[1]
    fetch = pltpu.make_async_copy(
        queries_ref.at[:, pl.ds(pl.multiple_of(quarter * cut, cut), cut)], mine_ref, sem
    )
    fetch.start()
    weights = weights_ref[...]
    slot_grad = slot_ref[...]
    centered = slot_grad - jnp.sum(weights * slot_grad, axis=0, keepdims=True)
    score_ref[...] = weights * centered
    dests = out_ref.shape[0]
    own = subs // dests
    per = width // own
    layer = layer_ref[...]
    for half in range(halves):
        picks = picks_ref[half]
        merged = jnp.zeros((slots, tokens), f32)
        for slot in range(slots):
            same = picks == picks_ref[half, slot : slot + 1, :]
            merged = merged + jnp.where(same, score_ref[slot : slot + 1, :], 0.0)
        for start in range(0, subs, 16):
            pair = []
            for first in (start, start + 8):
                found = found_ref[half, first : first + 8, :]
                low, high = found & 7, found >> 3
                acc = jnp.zeros((8, tokens), f32)
                for group in range(slots // 8):
                    table = merged[group * 8 : group * 8 + 8]
                    got = jnp.take_along_axis(table, low, axis=0)
                    acc = jnp.where(high == group, got, acc)
                pair.append(acc)
            sub_ref[half, start : start + 16, :] = jnp.concatenate(pair, axis=0).astype(bf16)
        dquery = lax.dot_general(
            sub_ref[half], keys_ref[half], (((0,), (0,)), ((), ())), preferred_element_type=f32
        ).astype(bf16)
        proj = lax.dot_general(
            dquery, layer, (((0,), (0,)), ((), ())), preferred_element_type=f32
        ).astype(bf16)
        for at in range(per):
            out_ref[half * per + at, :own, :] = proj[at * own : at * own + own]
    fetch.wait()
    key = jnp.dot(sub_ref[quarter >> 1], mine_ref[...], preferred_element_type=f32).astype(bf16)
    for at in range(dests):
        out_ref[at, own:, :] = key[at * own : at * own + own]


def sum_kernel(first, parts_ref, out_ref):
    rows = slice(first, first + out_ref.shape[0])
    total = parts_ref[0, rows, :].astype(f32)
    for at in range(1, parts_ref.shape[0]):
        total = total + parts_ref[at, rows, :].astype(f32)
    out_ref[...] = total.astype(out_ref.dtype)


def join_kernel(own_ref, one_ref, two_ref, three_ref, out_ref):
    quarter = lax.axis_index("mem") & 3
    cut = own_ref.shape[1]
    for at, ref in enumerate((own_ref, one_ref, two_ref, three_ref)):
        there = quarter ^ at
        out_ref[there >> 1, :, pl.ds(pl.multiple_of((there & 1) * cut, cut), cut)] = ref[...].astype(f32)


def stay(x):
    return pltpu.with_memory_space_constraint(x, pltpu.HBM)


def swap(x, mask, count):
    return lax.ppermute(x, "mem", [(at, at ^ mask) for at in range(count)])


def step_body(grad_out, values, slot_rows, weights, sub_picks, queries, sub_keys, layer_input):
    groups = lax.axis_size("dp")
    mem_count = lax.axis_size("mem")
    tokens, width = grad_out.shape
    slots = slot_rows.shape[1]
    val_rows = values.shape[0]
    halves, subs, key_width = sub_keys.shape
    weights_t = weights.T
    rows_t = slot_rows.T
    picks_t = jnp.swapaxes(sub_picks, 1, 2)

    def along_x(x, shift):
        return lax.ppermute(
            x, "dp", [(at, at // SIDE * SIDE + (at + shift) % SIDE) for at in range(groups)]
        )

    def along_y(x, shift):
        return lax.ppermute(x, "dp", [(at, (at + shift * SIDE) % groups) for at in range(groups)])

    far_values = along_x(values, 2)
    sent, own_values = run(
        pack_kernel,
        [shape((tokens + slots, width), bf16), shape(values.shape, bf16)],
        [stay(x) for x in (grad_out, rows_t, weights_t, values)],
        scratch=(
            pltpu.VMEM((slots, tokens), jnp.int32),
            pltpu.VMEM((slots, tokens), f32),
            pltpu.SemaphoreType.DMA((4,)),
        ),
        far=(0, 1, 2, 3),
    )
    recv = [sent] + [along_y(sent, shift) for shift in (1, 2, 3)]
    all_values = [own_values, along_x(values, 1), far_values, along_x(values, 3)]

    def value_part(shifts, recv):
        return run(
            functools.partial(value_kernel, shifts),
            [shape((val_rows, width), bf16 if shift else f32) for shift in shifts],
            recv,
            scratch=(
                pltpu.VMEM((SIDE, slots, tokens), f32),
                pltpu.VMEM((SIDE, slots, tokens), f32),
                pltpu.VMEM((val_rows, SIDE * tokens), bf16),
                pltpu.VMEM((SIDE * tokens, width), bf16),
            ),
            flops=2 * 10**9,
            data=2**20,
        )

    two_away, one_away, three_away = value_part((2, 1, 3), recv)
    slot_parts = run(
        slot_kernel,
        [shape((slots, tokens), f32)] * SIDE,
        (*recv, *all_values),
        flops=10**9,
        data=2**20,
    )
    slot_parts, recv = lax.optimization_barrier((slot_parts, recv))
    back = [along_y(slot_parts[shift], shift) for shift in (1, 2, 3)]
    sums = [along_x(two_away, 2)]
    slot_grad = (slot_parts[0] + back[0]) + (back[1] + back[2])
    slot_grad, one_away, three_away = lax.optimization_barrier((slot_grad, one_away, three_away))

    one, two, three = (swap(slot_grad, mask, mem_count) for mask in (1, 2, 3))
    sums.append(along_x(one_away, 1))
    slot_grad = (slot_grad + one) + (two + three)
    slot_grad, three_away = lax.optimization_barrier((slot_grad, three_away))
    step = swap(slot_grad, 4, mem_count)
    sums.append(along_x(three_away, 3))
    slot_grad = slot_grad + step
    step = swap(slot_grad, 12, mem_count)
    (mine,) = value_part((0,), recv)
    found = run(
        find_kernel,
        shape((halves, subs, tokens), jnp.int32),
        (picks_t,),
        scratch=(pltpu.VMEM((slots, tokens), f32), pltpu.VMEM((slots, 16, tokens), bf16)),
        flops=2 * 10**9,
        data=2**20,
    )
    slot_grad = slot_grad + step

    own = subs // groups
    parts = run(
        part_kernel,
        shape((groups, 2 * own, width), bf16),
        (slot_grad, weights_t, picks_t, found, queries, sub_keys, layer_input),
        scratch=(
            pltpu.VMEM((slots, tokens), f32),
            pltpu.VMEM((halves, subs, tokens), bf16),
            pltpu.VMEM((tokens, queries.shape[1] // 4), bf16),
            pltpu.SemaphoreType.DMA(()),
        ),
        far=(4,),
    )
    parts, mine, *sums = lax.optimization_barrier((parts, mine, *sums))
    parts = lax.all_to_all(parts, "dp", 0, 0, tiled=True)
    key = run(functools.partial(sum_kernel, own), shape((own, width), bf16), (parts,))
    key, mine, *sums = lax.optimization_barrier((key, mine, *sums))
    others = [swap(key, mask, mem_count) for mask in (1, 2, 3)]
    proj_grad = run(
        functools.partial(sum_kernel, 0),
        shape((own, width), f32),
        (parts,),
        flops=10**9,
        data=2**19,
    )
    value_grad = run(
        add_kernel, shape((val_rows, width), f32), (mine, *sums), flops=10**9, data=2**19
    )
    key_grad = run(join_kernel, shape((halves, own, key_width), f32), (key, *others))
    return (value_grad, key_grad, proj_grad)


def solution(mesh):
    return jax.shard_map(
        step_body,
        mesh=mesh,
        in_specs=(
            P("dp", "mem"),
            P("dp", "mem"),
            P("dp", None),
            P("dp", None),
            P(None, "dp", None),
            P("dp", None),
            P(),
            P("dp", "mem"),
        ),
        out_specs=(P("dp", "mem"), P(None, "dp", None), P("dp", "mem")),
        check_vma=False,
    )
```
